768 devices in a mesh: row: 2 (over core), sec: 24 (over z_lo, y), span: 16 (over x, z_hi).
Axes of the slice: x: 4, y: 8, z: 12 (z_hi: 4, z_lo: 3; z = z_hi * 3 + z_lo), core: 2. Of those that a mesh axis runs over, the one named last changes fastest.
Arguments:
- state: float32 [2, 9, 7, 4, 64, 3072], P('row', None, None, None, 'span', 'sec'), may hold values from -6 to 6
- viscosity: float32 [2, 4, 64, 3072], P('row', None, 'span', 'sec'), may hold values from 0.1 to 1
- jacobian: float32 [2, 7, 7], P('row'), may hold values from -2 to 2
- frequency: float32 [2], P('row'), may hold values from 0.5 to 2
- offsets: int32 [9], replicated, may hold values from 0 to 3071
Outputs:
- updated: float32 [2, 9, 7, 4, 64, 3072], P('row', None, None, None, 'span', 'sec')
The draws below stay inside these ranges and needn't reach their ends.
All inputs are finite; a program needn't handle non-finite values.
Results may differ from the reference program's by a relative error of at most 0.0001.
Values sent between devices are 32-bit elements; how exact they have to be, the bound alone decides.
A program may use at most 192 MiB of HBM per device.

```python
import math
import jax
import jax.numpy as jnp
from jax import lax

INSTANCES = 9
FIELDS = 7
AXIAL = 4
ROWS = 2
NS = 64
NT = 3072


def touch_ends(drawn, stream_key, low, high):
    place = [jax.random.randint(jax.random.fold_in(stream_key, axis), (), 0, length) for axis, length in enumerate(drawn.shape)]
    widest = drawn.shape.index(max(drawn.shape))
    next_to = place[:widest] + [(place[widest] + 1) % drawn.shape[widest]] + place[widest + 1:]
    return drawn.at[tuple(place)].set(low).at[tuple(next_to)].set(high)


def block_scale(stream_key, dims, cuts, least, top_value):
    def one(dim, blocks):
        heights = jax.random.uniform(jax.random.fold_in(jax.random.fold_in(stream_key, 6), dim), (blocks,), jnp.float32, least / len(cuts), top_value / len(cuts))
        return jnp.repeat(jnp.exp(heights), dims[dim] // blocks).reshape((-1,) + (1,) * (len(dims) - dim - 1))

    loudness = one(*cuts[0])
    for cut in cuts[1:]:
        loudness = loudness * one(*cut)
    return loudness


def noise(stream_key, dims, spread, most, shards=(), dtype=jnp.bfloat16):
    gain = block_scale(stream_key, dims, shards, -0.22, 0.18) if shards else 1.0
    values = jax.random.normal(stream_key, dims, jnp.float32) * spread * gain
    return jnp.minimum(jnp.maximum(values, -most), most).astype(dtype)


def setup_inputs(seed: int = 0) -> dict:
    arg_keys = jax.random.split(jax.random.key(seed), 6)
    return {
        "state": noise(arg_keys[0], (ROWS, INSTANCES, FIELDS, AXIAL, NS, NT), 1.0, 6.0, ((0, 2), (4, 16), (5, 24)), jnp.float32),
        "viscosity": jnp.clip(jnp.exp(math.log(1.0) - 2.3025851 * jax.random.uniform(arg_keys[1], (ROWS, AXIAL, NS, NT), jnp.float32) ** block_scale(arg_keys[1], (ROWS, AXIAL, NS, NT), ((0, 2), (2, 16), (3, 24)), -0.2, 0.2)), 0.1, 1.0),
        "jacobian": noise(arg_keys[2], (ROWS, FIELDS, FIELDS), FIELDS ** -0.5, 2.0, ((0, 2),), jnp.float32),
        "frequency": jnp.clip(jnp.exp(math.log(2.0) - 1.3862944 * jax.random.uniform(arg_keys[3], (ROWS,), jnp.float32) ** block_scale(arg_keys[3], (ROWS,), ((0, 2),), -0.2, 0.2)), 0.5, 2.0),
        "offsets": touch_ends(jax.random.randint(arg_keys[4], (INSTANCES,), 0, NT), jax.random.fold_in(arg_keys[4], 1), 0, NT - 1).astype(jnp.int32),
    }


def spectral_matrix(count):
    index = jnp.arange(count)
    offset = index[:, None] - index[None, :]
    parity = jnp.where(jnp.abs(offset) % 2 == 0, 1.0, -1.0).astype(jnp.float32)
    angle = (math.pi / count) * offset.astype(jnp.float32)
    safe_sin = jnp.where(offset == 0, jnp.float32(1.0), jnp.sin(angle))
    return jnp.where(offset == 0, jnp.float32(0.0), 0.5 * parity / safe_sin).astype(jnp.float32)


def reference(state, viscosity, jacobian, frequency, offsets):
    deriv = spectral_matrix(INSTANCES)
    collected_outputs = []
    for which in range(2):
        flow_field_values = state[which]
        other = state[1 - which][:, :, -1]
        if which == 0:
            shift = offsets
        else:
            shift = (NT - offsets) % NT
        ghost = jax.vmap(lambda block, amount: jnp.roll(block, amount, axis=-1))(other, shift)
        plus_theta = jnp.roll(flow_field_values, -1, axis=-1)
        minus_theta = jnp.roll(flow_field_values, 1, axis=-1)
        padded = jnp.pad(flow_field_values, ((0, 0), (0, 0), (0, 0), (1, 1), (0, 0)))
        upper_spanwise_neighbour = padded[:, :, :, 2:]
        lower_spanwise_neighbour = padded[:, :, :, :-2]
        plus_axial = jnp.concatenate([flow_field_values[:, :, 1:], ghost[:, :, None]], axis=2)
        minus_axial = jnp.concatenate([jnp.zeros_like(flow_field_values[:, :, :1]), flow_field_values[:, :, :-1]], axis=2)
        timeterm = jnp.einsum("tu,ufasc->tfasc", deriv, flow_field_values, precision=lax.Precision.HIGHEST)
        convect = jnp.einsum("fg,tgasc->tfasc", jacobian[which], plus_theta - minus_theta, precision=lax.Precision.HIGHEST)
        coeff = viscosity[which]
        residual = (-frequency[which] * timeterm - 0.5 * convect
                    + coeff * (plus_theta + minus_theta - 2.0 * flow_field_values)
                    + coeff * (upper_spanwise_neighbour + lower_spanwise_neighbour - 2.0 * flow_field_values)
                    + (plus_axial + minus_axial - 2.0 * flow_field_values))
        collected_outputs.append(flow_field_values + 0.1 * residual)
    return jnp.stack(collected_outputs)
```

```python
import functools
import math

import jax
import jax.numpy as jnp
from jax import lax
from jax.experimental import pallas as pl
from jax.experimental.pallas import tpu as pltpu
from jax.sharding import PartitionSpec as P

MESH = pl.DeviceIdType.MESH
LANES = 128


def kernel(
    sectors, slabs, times, fields, share,
    strip_src, state_src, visc_src, jac, freq, offs, out,
    state, strip, coeff, total,
    edge_up, edge_down, from_up, from_down,
    edges, edges_left, edges_right,
    gathered, turned, ghost,
    load_sem, send_sem, recv_sem,
):
    row = lax.axis_index("row")
    me = lax.axis_index("sec")
    slab = lax.axis_index("span")
    planes = times * fields
    holders = planes // share
    cells = planes * 4
    annulus = sectors * LANES

    loads = (
        pltpu.make_async_copy(strip_src.at[:, 3], strip, load_sem.at[0]),
        pltpu.make_async_copy(state_src, state, load_sem.at[1]),
        pltpu.make_async_copy(visc_src, coeff, load_sem.at[2]),
    )
    for load in loads:
        load.start()

    right = lax.rem(me + 1, sectors)
    left = lax.rem(me + (sectors - 1), sectors)
    has_up = slab < slabs - 1
    has_down = slab > 0

    barrier = pltpu.get_barrier_semaphore()

    @pl.loop(0, sectors)
    def _(step):
        target = lax.rem(me + step, sectors)
        pl.semaphore_signal(
            barrier, inc=1, device_id={"row": 1 - row, "sec": target}, device_id_type=MESH
        )

        @pl.when(step > 0)
        def _():
            pl.semaphore_signal(
                barrier, inc=1, device_id={"sec": target}, device_id_type=MESH
            )

    @pl.when(has_up)
    def _():
        pl.semaphore_signal(barrier, inc=1, device_id={"span": slab + 1}, device_id_type=MESH)

    @pl.when(has_down)
    def _():
        pl.semaphore_signal(barrier, inc=1, device_id={"span": slab - 1}, device_id_type=MESH)

    for load in loads:
        load.wait()

    edge_up[...] = state[pl.ds(3, cells, stride=4), :]
    edge_down[...] = state[pl.ds(0, cells, stride=4), :]
    lane = lax.broadcasted_iota(jnp.int32, (8, LANES), 1)
    sub = lax.broadcasted_iota(jnp.int32, (8, LANES), 0)

    def rows_of(t, f, half):
        return pl.ds(pl.multiple_of(t * (fields * 16) + (f * 16 + half * 8), 8), 8)

    def pack(t, held):
        packed = []
        for half in range(2):
            part = jnp.zeros((8, LANES), jnp.float32)
            for f in range(fields):
                turn = pltpu.roll(state[rows_of(t, f, half), :], 2 * f + 1, 1)
                part = jnp.where((lane >> 1) == f, turn, part)
            packed.append(held[half] + pltpu.roll(part, t * (2 * fields), 1))
        return tuple(packed)

    zero = jnp.zeros((8, LANES), jnp.float32)
    packed = lax.fori_loop(0, times, pack, (zero, zero))
    edges[pl.ds(0, 8), :] = packed[0]
    edges[pl.ds(8, 8), :] = packed[1]

    pl.semaphore_wait(
        barrier, 2 * sectors - 1 + has_up.astype(jnp.int32) + has_down.astype(jnp.int32)
    )

    @pl.loop(0, sectors)
    def _(step):
        target = lax.rem(me + step, sectors)

        @pl.when(target < holders)
        def _():
            pltpu.make_async_remote_copy(
                src_ref=strip.at[pl.ds(share * target, share)],
                dst_ref=gathered.at[me],
                send_sem=send_sem.at[0],
                recv_sem=recv_sem.at[0],
                device_id={"row": 1 - row, "sec": target},
                device_id_type=MESH,
            ).start()

    to_right = pltpu.make_async_remote_copy(
        src_ref=edges, dst_ref=edges_left, send_sem=send_sem.at[1], recv_sem=recv_sem.at[1],
        device_id={"sec": right}, device_id_type=MESH,
    )
    to_left = pltpu.make_async_remote_copy(
        src_ref=edges, dst_ref=edges_right, send_sem=send_sem.at[2], recv_sem=recv_sem.at[2],
        device_id={"sec": left}, device_id_type=MESH,
    )
    to_right.start()
    to_left.start()
    to_up = pltpu.make_async_remote_copy(
        src_ref=edge_up, dst_ref=from_down, send_sem=send_sem.at[3], recv_sem=recv_sem.at[3],
        device_id={"span": slab + 1}, device_id_type=MESH,
    )
    to_down = pltpu.make_async_remote_copy(
        src_ref=edge_down, dst_ref=from_up, send_sem=send_sem.at[4], recv_sem=recv_sem.at[4],
        device_id={"span": slab - 1}, device_id_type=MESH,
    )

    @pl.when(has_up)
    def _():
        to_up.start()

    @pl.when(has_down)
    def _():
        to_down.start()

    weights = [
        freq[0] * jnp.float32(-0.05 * (-1.0) ** m / math.sin(math.pi * m / times))
        for m in range(1, times // 2 + 1)
    ]

    @pl.loop(0, fields)
    def _(f):
        for half in range(2):
            at = [
                pl.ds(pl.multiple_of(f * 16 + (t * fields * 16 + half * 8), 8), 8)
                for t in range(times)
            ]
            values = [state[at[t], :] for t in range(times)]
            for t in range(times):
                acc = None
                for m, weight in enumerate(weights, 1):
                    term = weight * (values[(t - m) % times] - values[(t + m) % times])
                    acc = term if acc is None else acc + term
                total[at[t], :] = acc

    @pl.when(me < holders)
    def _():
        pltpu.make_async_copy(gathered, gathered, recv_sem.at[0]).wait()
        thin = lax.broadcasted_iota(jnp.int32, (4, LANES), 1)
        for part in range(share):
            offset = offs[(share * me + part) // fields]
            shift = jnp.where(row == 0, offset, annulus - offset)
            whole = shift >> 7
            rest = shift & (LANES - 1)
            before = pltpu.roll(
                gathered[lax.rem(2 * sectors - 1 - whole, sectors), part], rest, 1
            )
            for sector in range(sectors):
                after = pltpu.roll(
                    gathered[lax.rem(2 * sectors + sector - whole, sectors), part], rest, 1
                )
                turned[sector, part] = jnp.where(thin >= rest, after, before)
                before = after
        pltpu.make_async_copy(
            turned.at[me], ghost.at[pl.ds(share * me, share)], recv_sem.at[5]
        ).start()

        @pl.loop(1, sectors)
        def _(step):
            target = lax.rem(me + step, sectors)
            pltpu.make_async_remote_copy(
                src_ref=turned.at[target],
                dst_ref=ghost.at[pl.ds(share * me, share)],
                send_sem=send_sem.at[5],
                recv_sem=recv_sem.at[5],
                device_id={"sec": target},
                device_id_type=MESH,
            ).start()

    to_right.wait_recv()
    to_left.wait_recv()
    mix = [[jac[f, 0, g] * jnp.float32(-0.05) for g in range(fields)] for f in range(fields)]
    diffuse = [coeff[pl.ds(8 * half, 8), :] * jnp.float32(0.1) for half in range(2)]
    first_span = (sub & 3) == 0
    last_span = (sub & 3) == 3
    low = sub < 4

    @pl.loop(0, times)
    def _(t):
        turn = lax.rem(LANES - t * (2 * fields), LANES)
        lefts = [pltpu.roll(edges_left[pl.ds(8 * h, 8), :], turn, 1) for h in range(2)]
        rights = [pltpu.roll(edges_right[pl.ds(8 * h, 8), :], turn, 1) for h in range(2)]
        slopes = []
        for f in range(fields):
            pair = [state[rows_of(t, f, half), :] for half in range(2)]
            swapped = [pltpu.roll(v, 4, 0) for v in pair]
            middle = jnp.where(low, swapped[0], swapped[1])
            axial = (
                middle + jnp.where(low, 0.0, swapped[0]),
                middle + jnp.where(low, swapped[1], 0.0),
            )
            slope = []
            for half in range(2):
                v = pair[half]
                plus = jnp.where(
                    lane == LANES - 1,
                    pltpu.roll(rights[half], (LANES - 2 - 2 * f) % LANES, 1),
                    pltpu.roll(v, LANES - 1, 1),
                )
                minus = jnp.where(
                    lane == 0,
                    pltpu.roll(lefts[half], (LANES - 2 * f) % LANES, 1),
                    pltpu.roll(v, 1, 1),
                )
                around = plus + minus
                slope.append(plus - minus)
                around = around + jnp.where(last_span, 0.0, pltpu.roll(v, 7, 0))
                around = around + jnp.where(first_span, 0.0, pltpu.roll(v, 1, 0))
                at = rows_of(t, f, half)
                total[at, :] = (
                    total[at, :]
                    + 0.8 * v
                    + 0.1 * axial[half]
                    + diffuse[half] * (around - 4.0 * v)
                )
            slopes.append(slope)
        for f in range(fields):
            for half in range(2):
                acc = mix[f][0] * slopes[0][half]
                for g in range(1, fields):
                    acc = acc + mix[f][g] * slopes[g][half]
                at = rows_of(t, f, half)
                total[at, :] = total[at, :] + acc

    def span_weights(s):
        rows = [coeff[pl.ds(4 * a + s, 1), :] * jnp.float32(0.1) for a in range(4)]
        out = jnp.broadcast_to(rows[3], (8, LANES))
        for a in range(3):
            out = jnp.where((sub & 3) == a, jnp.broadcast_to(rows[a], (8, LANES)), out)
        return out

    def add_span(source, s):
        weight = span_weights(s)
        whole = cells // 8
        for block in range(whole):
            at = pl.ds(block * 32 + s, 8, stride=4)
            total[at, :] = total[at, :] + weight * source[pl.ds(block * 8, 8), :]
        if cells % 8:
            at = pl.ds(whole * 32 + s, cells % 8, stride=4)
            total[at, :] = (
                total[at, :]
                + weight[: cells % 8] * source[pl.ds(whole * 8, cells % 8), :]
            )

    @pl.when(has_up)
    def _():
        to_down.wait_recv()
        add_span(from_up, 3)

    @pl.when(has_down)
    def _():
        to_up.wait_recv()
        add_span(from_down, 0)

    pltpu.make_async_copy(ghost, ghost, recv_sem.at[5]).wait()
    for n in range(planes):
        at = pl.ds(16 * n + 12, 4)
        total[at, :] = total[at, :] + 0.1 * ghost[n]

    store = pltpu.make_async_copy(total, out, load_sem.at[0])
    store.start()
    pltpu.make_async_copy(strip, strip, send_sem.at[0]).wait()
    to_right.wait_send()
    to_left.wait_send()

    @pl.when(has_up)
    def _():
        to_up.wait_send()

    @pl.when(has_down)
    def _():
        to_down.wait_send()

    @pl.when(me < holders)
    def _():
        others = turned.at[pl.ds(0, sectors - 1)]
        pltpu.make_async_copy(others, others, send_sem.at[5]).wait()

    store.wait()


def solution(mesh):
    sectors, slabs = mesh.shape["sec"], mesh.shape["span"]

    def on_device(state, viscosity, jacobian, frequency, offsets):
        _, times, fields, axial, span, lanes = state.shape
        planes = times * fields
        share = next(
            s for s in range(-(-planes // sectors), planes + 1) if planes % s == 0
        )
        rows = planes * axial * span
        edge = pltpu.VMEM((planes * axial, lanes), jnp.float32)
        pairs = pltpu.VMEM((16, lanes), jnp.float32)
        anywhere = pl.BlockSpec(memory_space=pl.ANY)
        scalars = pl.BlockSpec(memory_space=pltpu.SMEM)
        out = pl.pallas_call(
            functools.partial(kernel, sectors, slabs, times, fields, share),
            out_shape=jax.ShapeDtypeStruct((rows, lanes), jnp.float32),
            in_specs=[anywhere] * 3 + [scalars] * 3,
            out_specs=anywhere,
            scratch_shapes=[
                pltpu.VMEM((rows, lanes), jnp.float32),
                pltpu.VMEM((planes, span, lanes), jnp.float32),
                pltpu.VMEM((16, lanes), jnp.float32),
                pltpu.VMEM((rows, lanes), jnp.float32),
                edge, edge, edge, edge,
                pairs, pairs, pairs,
                pltpu.VMEM((sectors, share, span, lanes), jnp.float32),
                pltpu.VMEM((sectors, share, span, lanes), jnp.float32),
                pltpu.VMEM((planes, span, lanes), jnp.float32),
                pltpu.SemaphoreType.DMA((3,)),
                pltpu.SemaphoreType.DMA((6,)),
                pltpu.SemaphoreType.DMA((6,)),
            ],
            compiler_params=pltpu.CompilerParams(collective_id=0, has_side_effects=True),
        )(
            state.reshape(planes, axial, span, lanes),
            state.reshape(rows, lanes),
            viscosity.reshape(axial * span, lanes),
            jacobian.reshape(fields, 1, fields),
            frequency,
            offsets,
        )
        return out.reshape(state.shape)

    return jax.shard_map(
        on_device,
        mesh=mesh,
        in_specs=(
            P("row", None, None, None, "span", "sec"),
            P("row", None, "span", "sec"),
            P("row", None, None),
            P("row"),
            P(),
        ),
        out_specs=P("row", None, None, None, "span", "sec"),
        check_vma=False,
    )
```

```python
import functools
import math

import jax
import jax.numpy as jnp
from jax import lax
from jax.experimental import pallas as pl
from jax.experimental.pallas import tpu as pltpu
from jax.sharding import PartitionSpec as P

MESH = pl.DeviceIdType.MESH
LANES = 128
DEPTHS = 4
AWAY = (0, 12, 20)


def kernel(
    sectors, slabs, times, fields, share, away,
    strip_src, state_src, visc_src, jac_src, freq_src, offs_src, total,
    state, coeff, jac, freq, offs,
    edge_up, edge_down, from_up, from_down,
    edges, edges_left, edges_right,
    gathered, turned, ghost,
    load_sem, send_sem, recv_sem, ready_sem, home_sem,
):
    row = lax.axis_index("row")
    me = lax.axis_index("sec")
    slab = lax.axis_index("span")
    planes = times * fields
    cells = planes * 4
    annulus = sectors * LANES

    right = lax.rem(me + 1, sectors)
    left = lax.rem(me + (sectors - 1), sectors)

    def is_holder(sector):
        held = sector != away[0]
        for other in away[1:]:
            held = held & (sector != other)
        return held

    def rank(sector):
        before = sector
        for other in away:
            before = before - jnp.where(sector > other, 1, 0)
        return before

    is_home = is_holder(me)
    mine = rank(me)

    depth = lax.rem(slab, DEPTHS)
    ordered = depth == DEPTHS - 1
    is_root = (row == 0) & (me == 0) & (slab == 0)

    def lateness(at_row, sector):
        along = sector & 7
        late = 10 * jnp.minimum(along, 8 - along) + jnp.where(along > 3, 10, 0) + jnp.where(sector > 15, 14, 0)
        return late * (2 * sectors) + 2 * sector + at_row

    here = lateness(row, me)

    def root_at(at_row, sector):
        return (at_row == 0) & (sector == 0) & (slab == 0)

    def is_later(at_row, sector):
        return root_at(at_row, sector) | (ordered & ~is_root & (lateness(at_row, sector) > here))

    targets = [lax.rem(me + step, sectors) for step in range(sectors)]
    across_later = [is_later(1 - row, target) for target in targets]
    along_later = [is_later(row, target) for target in targets]
    across_tell = [(ordered & ~later) | is_root for later in across_later]
    along_tell = [(ordered & ~later) | is_root for later in along_later]

    has_up = slab < slabs - 1
    has_down = slab > 0
    over_root = (row == 0) & (me == 0) & (slab == 1)
    wrap_up = has_up & (depth == DEPTHS - 1)
    wrap_down = has_down & (depth == 0)
    down_later = wrap_down | over_root
    right_later = along_later[1]
    left_later = along_later[sectors - 1]
    neighbours = (
        (has_up, wrap_up | is_root, None, {"span": slab + 1}, 0, 1),
        (has_down & ~down_later, None, down_later, {"span": slab - 1}, 1, 0),
        (~right_later, along_tell[1], right_later, {"sec": targets[1]}, 2, 3),
        (~left_later, along_tell[sectors - 1], left_later, {"sec": targets[sectors - 1]}, 3, 2),
    )

    barrier = pltpu.get_barrier_semaphore()

    def signal(sem, device):
        pl.semaphore_signal(sem, inc=1, device_id=device, device_id_type=MESH)

    def count(flags):
        return sum(flag.astype(jnp.int32) for flag in flags)

    for step, target in enumerate(targets):
        pl.when(across_later[step] | ~across_tell[step])(
            functools.partial(signal, barrier, {"row": 1 - row, "sec": target})
        )
        if step:
            pl.when(along_later[step] | ~along_tell[step])(
                functools.partial(signal, barrier, {"sec": target})
            )
    pl.when(has_up & ~wrap_up & ~is_root)(
        functools.partial(signal, barrier, {"span": slab + 1})
    )
    pl.when(has_down)(functools.partial(signal, barrier, {"span": slab - 1}))

    loads = (
        pltpu.make_async_copy(state_src, state, load_sem.at[0]),
        pltpu.make_async_copy(visc_src, coeff, load_sem.at[1]),
        pltpu.make_async_copy(jac_src, jac, load_sem.at[2]),
        pltpu.make_async_copy(freq_src, freq, load_sem.at[3]),
        pltpu.make_async_copy(offs_src, offs, load_sem.at[4]),
    )
    for load in loads:
        load.start()

    pl.semaphore_wait(
        barrier,
        2 * sectors
        - 1
        - count(across_later)
        - count(along_later[1:])
        + count((neighbours[0][0], neighbours[1][0])),
    )
    for _, told, _, device, _, there in neighbours:
        if told is not None:
            pl.when(told)(functools.partial(signal, ready_sem.at[there], device))

    def spread(chosen):
        for step, target in enumerate(targets):

            @pl.when(is_holder(target) & chosen[step])
            def _(target=target):
                pltpu.make_async_remote_copy(
                    src_ref=strip_src.at[pl.ds(share * rank(target), share), 3],
                    dst_ref=gathered.at[me],
                    send_sem=send_sem.at[0],
                    recv_sem=recv_sem.at[0],
                    device_id={"row": 1 - row, "sec": target},
                    device_id_type=MESH,
                ).start()

    @pl.when(is_home)
    def _():
        for step, target in enumerate(targets):
            pl.when(across_tell[step])(
                functools.partial(signal, home_sem.at[0], {"row": 1 - row, "sec": target})
            )

    spread([~later for later in across_later])
    for step in range(1, sectors):
        pl.when(along_tell[step] & is_holder(targets[step]))(
            functools.partial(signal, home_sem.at[1], {"sec": targets[step]})
        )

    for load in loads:
        load.wait()

    edge_up[...] = state[pl.ds(3, cells, stride=4), :]
    edge_down[...] = state[pl.ds(0, cells, stride=4), :]
    to_right = pltpu.make_async_remote_copy(
        src_ref=edges, dst_ref=edges_left, send_sem=send_sem.at[1], recv_sem=recv_sem.at[1],
        device_id={"sec": targets[1]}, device_id_type=MESH,
    )
    to_left = pltpu.make_async_remote_copy(
        src_ref=edges, dst_ref=edges_right, send_sem=send_sem.at[2], recv_sem=recv_sem.at[2],
        device_id={"sec": targets[sectors - 1]}, device_id_type=MESH,
    )
    to_up = pltpu.make_async_remote_copy(
        src_ref=edge_up, dst_ref=from_down, send_sem=send_sem.at[3], recv_sem=recv_sem.at[3],
        device_id={"span": slab + 1}, device_id_type=MESH,
    )
    to_down = pltpu.make_async_remote_copy(
        src_ref=edge_down, dst_ref=from_up, send_sem=send_sem.at[4], recv_sem=recv_sem.at[4],
        device_id={"span": slab - 1}, device_id_type=MESH,
    )
    halos = tuple(zip((to_up, to_down, to_right, to_left), neighbours))
    for halo, (earlier, _, _, _, _, _) in halos[:2]:
        pl.when(earlier)(halo.start)

    lane = lax.broadcasted_iota(jnp.int32, (8, LANES), 1)
    sub = lax.broadcasted_iota(jnp.int32, (8, LANES), 0)

    def rows_of(t, f, half):
        return pl.ds(pl.multiple_of(t * (fields * 16) + (f * 16 + half * 8), 8), 8)

    def pack(t, held):
        packed = []
        for half in range(2):
            part = jnp.zeros((8, LANES), jnp.float32)
            for f in range(fields):
                turn = pltpu.roll(state[rows_of(t, f, half), :], 2 * f + 1, 1)
                part = jnp.where((lane >> 1) == f, turn, part)
            packed.append(held[half] + pltpu.roll(part, t * (2 * fields), 1))
        return tuple(packed)

    zero = jnp.zeros((8, LANES), jnp.float32)
    packed = lax.fori_loop(0, times, pack, (zero, zero))
    edges[pl.ds(0, 8), :] = packed[0]
    edges[pl.ds(8, 8), :] = packed[1]

    for halo, (earlier, _, _, _, _, _) in halos[2:]:
        pl.when(earlier)(halo.start)

    weights = [
        freq[0] * jnp.float32(-0.05 * (-1.0) ** m / math.sin(math.pi * m / times))
        for m in range(1, times // 2 + 1)
    ]

    @pl.loop(0, fields)
    def _(f):
        for half in range(2):
            at = [
                pl.ds(pl.multiple_of(f * 16 + (t * fields * 16 + half * 8), 8), 8)
                for t in range(times)
            ]
            values = [state[at[t], :] for t in range(times)]
            for t in range(times):
                acc = None
                for m, weight in enumerate(weights, 1):
                    term = weight * (values[(t - m) % times] - values[(t + m) % times])
                    acc = term if acc is None else acc + term
                total[at[t], :] = acc

    def send_later(index, now):
        halo, (_, _, later, _, told, _) = halos[index]

        @pl.when(later & now)
        def _():
            pl.semaphore_wait(ready_sem.at[told], 1)
            halo.start()

    across = count([later & is_holder(target) for later, target in zip(across_later, targets)])

    @pl.when(across > 0)
    def _():
        pl.semaphore_wait(home_sem.at[0], across)
        spread(across_later)

    beside_root = (row == 0) & (slab == 0)
    root_right = beside_root & (targets[1] == 0)
    root_left = beside_root & (targets[sectors - 1] == 0)
    send_later(2, ~root_right)
    send_later(3, ~root_left)

    @pl.when(is_home)
    def _():
        pltpu.make_async_copy(gathered, gathered, recv_sem.at[0]).wait()
        along = count(along_later[1:])

        @pl.when(along > 0)
        def _():
            pl.semaphore_wait(home_sem.at[1], along)

        thin = lax.broadcasted_iota(jnp.int32, (4, LANES), 1)
        wholes, rests = [], []
        for part in range(share):
            offset = offs[(share * mine + part) // fields]
            shift = jnp.where(row == 0, offset, annulus - offset)
            wholes.append(shift >> 7)
            rests.append(shift & (LANES - 1))

        def source(sector, part):
            at = lax.rem(sector + (2 * sectors - wholes[part]), sectors)
            return pltpu.roll(gathered[at, part], rests[part], 1)

        before = [source(me - 1, part) for part in range(share)]
        there = ghost.at[pl.ds(share * mine, share)]
        for step in range(sectors):
            target = lax.rem(me + step, sectors)
            for part in range(share):
                after = source(me + step, part)
                turned[target, part] = jnp.where(thin >= rests[part], after, before[part])
                before[part] = after
            if step == 0:
                pltpu.make_async_copy(turned.at[me], there, recv_sem.at[5]).start()
            else:
                pltpu.make_async_remote_copy(
                    src_ref=turned.at[target],
                    dst_ref=there,
                    send_sem=send_sem.at[5],
                    recv_sem=recv_sem.at[5],
                    device_id={"sec": target},
                    device_id_type=MESH,
                ).start()

    send_later(2, root_right)
    send_later(3, root_left)
    send_later(1, has_down)

    to_right.wait_recv()
    to_left.wait_recv()
    mix = [[jac[f, 0, g] * jnp.float32(-0.05) for g in range(fields)] for f in range(fields)]
    diffuse = [coeff[pl.ds(8 * half, 8), :] * jnp.float32(0.1) for half in range(2)]
    first_span = (sub & 3) == 0
    last_span = (sub & 3) == 3
    low = sub < 4

    @pl.loop(0, times)
    def _(t):
        turn = lax.rem(LANES - t * (2 * fields), LANES)
        lefts = [pltpu.roll(edges_left[pl.ds(8 * h, 8), :], turn, 1) for h in range(2)]
        rights = [pltpu.roll(edges_right[pl.ds(8 * h, 8), :], turn, 1) for h in range(2)]
        slopes = []
        for f in range(fields):
            pair = [state[rows_of(t, f, half), :] for half in range(2)]
            swapped = [pltpu.roll(v, 4, 0) for v in pair]
            middle = jnp.where(low, swapped[0], swapped[1])
            axial = (
                middle + jnp.where(low, 0.0, swapped[0]),
                middle + jnp.where(low, swapped[1], 0.0),
            )
            slope = []
            for half in range(2):
                v = pair[half]
                plus = jnp.where(
                    lane == LANES - 1,
                    pltpu.roll(rights[half], (LANES - 2 - 2 * f) % LANES, 1),
                    pltpu.roll(v, LANES - 1, 1),
                )
                minus = jnp.where(
                    lane == 0,
                    pltpu.roll(lefts[half], (LANES - 2 * f) % LANES, 1),
                    pltpu.roll(v, 1, 1),
                )
                around = plus + minus
                slope.append(plus - minus)
                around = around + jnp.where(last_span, 0.0, pltpu.roll(v, 7, 0))
                around = around + jnp.where(first_span, 0.0, pltpu.roll(v, 1, 0))
                at = rows_of(t, f, half)
                total[at, :] = (
                    total[at, :]
                    + 0.8 * v
                    + 0.1 * axial[half]
                    + diffuse[half] * (around - 4.0 * v)
                )
            slopes.append(slope)
        for f in range(fields):
            for half in range(2):
                acc = mix[f][0] * slopes[0][half]
                for g in range(1, fields):
                    acc = acc + mix[f][g] * slopes[g][half]
                at = rows_of(t, f, half)
                total[at, :] = total[at, :] + acc

    def span_weights(s):
        rows = [coeff[pl.ds(4 * a + s, 1), :] * jnp.float32(0.1) for a in range(4)]
        out = jnp.broadcast_to(rows[3], (8, LANES))
        for a in range(3):
            out = jnp.where((sub & 3) == a, jnp.broadcast_to(rows[a], (8, LANES)), out)
        return out

    def add_span(source, s):
        weight = span_weights(s)
        whole = cells // 8
        for block in range(whole):
            at = pl.ds(block * 32 + s, 8, stride=4)
            total[at, :] = total[at, :] + weight * source[pl.ds(block * 8, 8), :]
        if cells % 8:
            at = pl.ds(whole * 32 + s, cells % 8, stride=4)
            total[at, :] = (
                total[at, :]
                + weight[: cells % 8] * source[pl.ds(whole * 8, cells % 8), :]
            )

    @pl.when(has_up)
    def _():
        to_down.wait_recv()
        add_span(from_up, 3)

    @pl.when(has_down)
    def _():
        to_up.wait_recv()
        add_span(from_down, 0)

    pltpu.make_async_copy(ghost, ghost, recv_sem.at[5]).wait()
    for n in range(planes):
        at = pl.ds(16 * n + 12, 4)
        total[at, :] = total[at, :] + 0.1 * ghost[n]

    pltpu.make_async_copy(ghost, ghost, send_sem.at[0]).wait()
    to_right.wait_send()
    to_left.wait_send()

    @pl.when(has_up)
    def _():
        to_up.wait_send()

    @pl.when(has_down)
    def _():
        to_down.wait_send()

    @pl.when(is_home)
    def _():
        others = turned.at[pl.ds(0, sectors - 1)]
        pltpu.make_async_copy(others, others, send_sem.at[5]).wait()


def solution(mesh):
    sectors, slabs = mesh.shape["sec"], mesh.shape["span"]

    def on_device(state, viscosity, jacobian, frequency, offsets):
        _, times, fields, axial, span, lanes = state.shape
        planes = times * fields
        share = planes // (sectors - len(AWAY))
        rows = planes * axial * span
        edge = pltpu.VMEM((planes * axial, lanes), jnp.float32)
        pairs = pltpu.VMEM((16, lanes), jnp.float32)
        anywhere = pl.BlockSpec(memory_space=pltpu.HBM)
        out = pl.pallas_call(
            functools.partial(kernel, sectors, slabs, times, fields, share, AWAY),
            out_shape=pltpu.VMEM((rows, lanes), jnp.float32),
            in_specs=[anywhere] * 6,
            out_specs=pl.BlockSpec(memory_space=pltpu.VMEM),
            scratch_shapes=[
                pltpu.VMEM((rows, lanes), jnp.float32),
                pltpu.VMEM((16, lanes), jnp.float32),
                pltpu.SMEM((fields, 1, fields), jnp.float32),
                pltpu.SMEM((1,), jnp.float32),
                pltpu.SMEM((times,), jnp.int32),
                edge, edge, edge, edge,
                pairs, pairs, pairs,
                pltpu.VMEM((sectors, share, span, lanes), jnp.float32),
                pltpu.VMEM((sectors, share, span, lanes), jnp.float32),
                pltpu.VMEM((planes, span, lanes), jnp.float32),
                pltpu.SemaphoreType.DMA((5,)),
                pltpu.SemaphoreType.DMA((6,)),
                pltpu.SemaphoreType.DMA((6,)),
                pltpu.SemaphoreType.REGULAR((4,)),
                pltpu.SemaphoreType.REGULAR((2,)),
            ],
            compiler_params=pltpu.CompilerParams(collective_id=0, has_side_effects=True),
        )(
            state.reshape(planes, axial, span, lanes),
            state.reshape(rows, lanes),
            viscosity.reshape(axial * span, lanes),
            jacobian.reshape(fields, 1, fields),
            frequency,
            offsets,
        )
        return out.reshape(state.shape)

    return jax.shard_map(
        on_device,
        mesh=mesh,
        in_specs=(
            P("row", None, None, None, "span", "sec"),
            P("row", None, "span", "sec"),
            P("row", None, None),
            P("row"),
            P(),
        ),
        out_specs=P("row", None, None, None, "span", "sec"),
        check_vma=False,
    )
```

```python
import functools
import math

import jax
import jax.numpy as jnp
from jax import lax
from jax.experimental import pallas as pl
from jax.experimental.pallas import tpu as pltpu
from jax.sharding import PartitionSpec as P

MESH = pl.DeviceIdType.MESH
LANES = 128
DEPTHS = 4
AWAY = (0, 12, 20)


def kernel(
    sectors, slabs, times, fields, share, away,
    strip_src, state_src, visc_src, jac_src, freq_src, offs_src, total,
    state, coeff, jac, freq, offs,
    edge_up, edge_down, from_up, from_down,
    edges, edges_left, edges_right,
    gathered, turned, ghost,
    load_sem, send_sem, recv_sem, ready_sem, home_sem,
):
    row = lax.axis_index("row")
    me = lax.axis_index("sec")
    slab = lax.axis_index("span")
    planes = times * fields
    cells = planes * 4
    annulus = sectors * LANES

    def is_holder(sector):
        held = sector != away[0]
        for other in away[1:]:
            held = held & (sector != other)
        return held

    def rank(sector):
        before = sector
        for other in away:
            before = before - jnp.where(sector > other, 1, 0)
        return before

    is_home = is_holder(me)
    mine = rank(me)

    depth = lax.rem(slab, DEPTHS)
    ordered = depth == DEPTHS - 1
    is_root = (row == 0) & (me == 0) & (slab == 0)

    def lateness(at_row, sector):
        along = sector & 7
        late = 10 * jnp.minimum(along, 8 - along) + jnp.where(along > 3, 10, 0) + jnp.where(sector > 15, 14, 0)
        return late * (2 * sectors) + 2 * sector + at_row

    here = lateness(row, me)

    def root_at(at_row, sector):
        return (at_row == 0) & (sector == 0) & (slab == 0)

    targets = [lax.rem(me + step, sectors) for step in range(sectors)]
    held = [is_holder(target) for target in targets]
    far_first = sorted(range(sectors), key=lambda step: -min(step % 8, 8 - step % 8))

    def choose(one, other):
        return (ordered & one) | (~ordered & other)

    across_later = [ordered & (lateness(1 - row, target) > here) for target in targets]
    along_later = [lateness(row, target) > here for target in targets]
    across_greet = [choose(later, is_home) for later in across_later]
    across_wait = [choose(~later, at) for later, at in zip(across_later, held)]
    along_greet, along_wait, along_tell, along_miss = [None], [None], [None], [None]
    for step in range(1, sectors):
        later, at = along_later[step], held[step]
        greet, wait = is_home & ~at, ~is_home & at
        if step in (1, sectors - 1):
            greet, wait = greet | ~is_root, wait | ~root_at(row, targets[step])
        along_greet.append(choose(later, greet))
        along_wait.append(choose(~later, wait))
        along_tell.append(choose(~later & at, ~is_home & at))
        along_miss.append(choose(later, is_home & ~at))

    has_up = slab < slabs - 1
    has_down = slab > 0
    up_later = has_up & (depth != DEPTHS - 1) & ~is_root
    up_earlier = has_up & ~up_later
    down_later = has_down & ((depth == 0) | ((row == 0) & (me == 0) & (slab == 1)))
    down_earlier = has_down & ~down_later

    def beside(step):
        root, later = root_at(row, targets[step]), along_later[step]
        return choose(~later, ~root), choose(~later, is_root), choose(later, root)

    neighbours = (
        (up_earlier, up_earlier, up_later, {"span": slab + 1}, 0, 1),
        (down_earlier, down_earlier, down_later, {"span": slab - 1}, 1, 0),
        (*beside(1), {"sec": targets[1]}, 2, 3),
        (*beside(sectors - 1), {"sec": targets[sectors - 1]}, 3, 2),
    )

    barrier = pltpu.get_barrier_semaphore()

    def signal(sem, device):
        pl.semaphore_signal(sem, inc=1, device_id=device, device_id_type=MESH)

    def count(flags):
        return sum(flag.astype(jnp.int32) for flag in flags)

    for step in far_first:
        pl.when(across_greet[step])(
            functools.partial(signal, barrier, {"row": 1 - row, "sec": targets[step]})
        )
    for step in far_first:
        if step:
            pl.when(along_greet[step])(
                functools.partial(signal, barrier, {"sec": targets[step]})
            )
    for _, _, later, device, _, _ in neighbours[:2]:
        pl.when(later)(functools.partial(signal, barrier, device))

    loads = (
        pltpu.make_async_copy(state_src, state, load_sem.at[0]),
        pltpu.make_async_copy(visc_src, coeff, load_sem.at[1]),
        pltpu.make_async_copy(jac_src, jac, load_sem.at[2]),
        pltpu.make_async_copy(freq_src, freq, load_sem.at[3]),
        pltpu.make_async_copy(offs_src, offs, load_sem.at[4]),
    )
    for load in loads:
        load.start()

    pl.semaphore_wait(
        barrier, count(across_wait + along_wait[1:] + [up_earlier, down_earlier])
    )
    for _, told, _, device, _, there in neighbours:
        pl.when(told)(functools.partial(signal, ready_sem.at[there], device))

    def spread(chosen):
        for step in far_first:

            @pl.when(held[step] & chosen[step])
            def _(target=targets[step]):
                pltpu.make_async_remote_copy(
                    src_ref=strip_src.at[pl.ds(share * rank(target), share), 3],
                    dst_ref=gathered.at[me],
                    send_sem=send_sem.at[0],
                    recv_sem=recv_sem.at[0],
                    device_id={"row": 1 - row, "sec": target},
                    device_id_type=MESH,
                ).start()

    @pl.when(is_home & ordered)
    def _():
        for step in far_first:
            pl.when(~across_later[step])(
                functools.partial(
                    signal, home_sem.at[0], {"row": 1 - row, "sec": targets[step]}
                )
            )

    spread([~later for later in across_later])
    for step in range(1, sectors):
        pl.when(along_tell[step])(
            functools.partial(signal, home_sem.at[1], {"sec": targets[step]})
        )

    for load in loads:
        load.wait()

    edge_up[...] = state[pl.ds(3, cells, stride=4), :]
    edge_down[...] = state[pl.ds(0, cells, stride=4), :]
    to_right = pltpu.make_async_remote_copy(
        src_ref=edges, dst_ref=edges_left, send_sem=send_sem.at[1], recv_sem=recv_sem.at[1],
        device_id={"sec": targets[1]}, device_id_type=MESH,
    )
    to_left = pltpu.make_async_remote_copy(
        src_ref=edges, dst_ref=edges_right, send_sem=send_sem.at[2], recv_sem=recv_sem.at[2],
        device_id={"sec": targets[sectors - 1]}, device_id_type=MESH,
    )
    to_up = pltpu.make_async_remote_copy(
        src_ref=edge_up, dst_ref=from_down, send_sem=send_sem.at[3], recv_sem=recv_sem.at[3],
        device_id={"span": slab + 1}, device_id_type=MESH,
    )
    to_down = pltpu.make_async_remote_copy(
        src_ref=edge_down, dst_ref=from_up, send_sem=send_sem.at[4], recv_sem=recv_sem.at[4],
        device_id={"span": slab - 1}, device_id_type=MESH,
    )
    halos = tuple(zip((to_up, to_down, to_right, to_left), neighbours))
    for halo, (earlier, _, _, _, _, _) in halos[:2]:
        pl.when(earlier)(halo.start)

    lane = lax.broadcasted_iota(jnp.int32, (8, LANES), 1)
    sub = lax.broadcasted_iota(jnp.int32, (8, LANES), 0)

    def rows_of(t, f, half):
        return pl.ds(pl.multiple_of(t * (fields * 16) + (f * 16 + half * 8), 8), 8)

    def pack(t, held):
        packed = []
        for half in range(2):
            part = jnp.zeros((8, LANES), jnp.float32)
            for f in range(fields):
                turn = pltpu.roll(state[rows_of(t, f, half), :], 2 * f + 1, 1)
                part = jnp.where((lane >> 1) == f, turn, part)
            packed.append(held[half] + pltpu.roll(part, t * (2 * fields), 1))
        return tuple(packed)

    zero = jnp.zeros((8, LANES), jnp.float32)
    packed = lax.fori_loop(0, times, pack, (zero, zero))
    edges[pl.ds(0, 8), :] = packed[0]
    edges[pl.ds(8, 8), :] = packed[1]

    for halo, (earlier, _, _, _, _, _) in halos[2:]:
        pl.when(earlier)(halo.start)

    weights = [
        freq[0] * jnp.float32(-0.05 * (-1.0) ** m / math.sin(math.pi * m / times))
        for m in range(1, times // 2 + 1)
    ]

    @pl.loop(0, fields)
    def _(f):
        for half in range(2):
            at = [
                pl.ds(pl.multiple_of(f * 16 + (t * fields * 16 + half * 8), 8), 8)
                for t in range(times)
            ]
            values = [state[at[t], :] for t in range(times)]
            for t in range(times):
                acc = None
                for m, weight in enumerate(weights, 1):
                    term = weight * (values[(t - m) % times] - values[(t + m) % times])
                    acc = term if acc is None else acc + term
                total[at[t], :] = acc

    def send_later(index, now):
        halo, (_, _, later, _, told, _) = halos[index]

        @pl.when(later & now)
        def _():
            pl.semaphore_wait(ready_sem.at[told], 1)
            halo.start()

    across = count([later & at for later, at in zip(across_later, held)])

    @pl.when(across > 0)
    def _():
        pl.semaphore_wait(home_sem.at[0], across)
        spread(across_later)

    beside_root = (row == 0) & (slab == 0)
    root_right = beside_root & (targets[1] == 0)
    root_left = beside_root & (targets[sectors - 1] == 0)
    send_later(2, ~root_right)
    send_later(3, ~root_left)
    soon = (depth == DEPTHS - 2) | (depth == DEPTHS - 3)
    send_later(0, soon)

    @pl.when(is_home)
    def _():
        pltpu.make_async_copy(gathered, gathered, recv_sem.at[0]).wait()
        along = count(along_miss[1:])

        @pl.when(along > 0)
        def _():
            pl.semaphore_wait(home_sem.at[1], along)

        thin = lax.broadcasted_iota(jnp.int32, (4, LANES), 1)
        wholes, rests = [], []
        for part in range(share):
            offset = offs[(share * mine + part) // fields]
            shift = jnp.where(row == 0, offset, annulus - offset)
            wholes.append(shift >> 7)
            rests.append(shift & (LANES - 1))

        def source(sector, part):
            at = lax.rem(sector + (2 * sectors - wholes[part]), sectors)
            return pltpu.roll(gathered[at, part], rests[part], 1)

        before = [source(me - 1, part) for part in range(share)]
        there = ghost.at[pl.ds(share * mine, share)]
        for step in range(sectors):
            target = lax.rem(me + step, sectors)
            for part in range(share):
                after = source(me + step, part)
                turned[target, part] = jnp.where(thin >= rests[part], after, before[part])
                before[part] = after
            if step == 0:
                pltpu.make_async_copy(turned.at[me], there, recv_sem.at[5]).start()
            else:
                pltpu.make_async_remote_copy(
                    src_ref=turned.at[target],
                    dst_ref=there,
                    send_sem=send_sem.at[5],
                    recv_sem=recv_sem.at[5],
                    device_id={"sec": target},
                    device_id_type=MESH,
                ).start()

    send_later(2, root_right)
    send_later(3, root_left)
    send_later(0, ~soon)
    send_later(1, has_down)

    to_right.wait_recv()
    to_left.wait_recv()
    mix = [[jac[f, 0, g] * jnp.float32(-0.05) for g in range(fields)] for f in range(fields)]
    diffuse = [coeff[pl.ds(8 * half, 8), :] * jnp.float32(0.1) for half in range(2)]
    first_span = (sub & 3) == 0
    last_span = (sub & 3) == 3
    low = sub < 4

    @pl.loop(0, times)
    def _(t):
        turn = lax.rem(LANES - t * (2 * fields), LANES)
        lefts = [pltpu.roll(edges_left[pl.ds(8 * h, 8), :], turn, 1) for h in range(2)]
        rights = [pltpu.roll(edges_right[pl.ds(8 * h, 8), :], turn, 1) for h in range(2)]
        slopes = []
        for f in range(fields):
            pair = [state[rows_of(t, f, half), :] for half in range(2)]
            swapped = [pltpu.roll(v, 4, 0) for v in pair]
            middle = jnp.where(low, swapped[0], swapped[1])
            axial = (
                middle + jnp.where(low, 0.0, swapped[0]),
                middle + jnp.where(low, swapped[1], 0.0),
            )
            slope = []
            for half in range(2):
                v = pair[half]
                plus = jnp.where(
                    lane == LANES - 1,
                    pltpu.roll(rights[half], (LANES - 2 - 2 * f) % LANES, 1),
                    pltpu.roll(v, LANES - 1, 1),
                )
                minus = jnp.where(
                    lane == 0,
                    pltpu.roll(lefts[half], (LANES - 2 * f) % LANES, 1),
                    pltpu.roll(v, 1, 1),
                )
                around = plus + minus
                slope.append(plus - minus)
                around = around + jnp.where(last_span, 0.0, pltpu.roll(v, 7, 0))
                around = around + jnp.where(first_span, 0.0, pltpu.roll(v, 1, 0))
                at = rows_of(t, f, half)
                total[at, :] = (
                    total[at, :]
                    + 0.8 * v
                    + 0.1 * axial[half]
                    + diffuse[half] * (around - 4.0 * v)
                )
            slopes.append(slope)
        for f in range(fields):
            for half in range(2):
                acc = mix[f][0] * slopes[0][half]
                for g in range(1, fields):
                    acc = acc + mix[f][g] * slopes[g][half]
                at = rows_of(t, f, half)
                total[at, :] = total[at, :] + acc

    def span_weights(s):
        rows = [coeff[pl.ds(4 * a + s, 1), :] * jnp.float32(0.1) for a in range(4)]
        out = jnp.broadcast_to(rows[3], (8, LANES))
        for a in range(3):
            out = jnp.where((sub & 3) == a, jnp.broadcast_to(rows[a], (8, LANES)), out)
        return out

    def add_span(source, s):
        weight = span_weights(s)
        whole = cells // 8
        for block in range(whole):
            at = pl.ds(block * 32 + s, 8, stride=4)
            total[at, :] = total[at, :] + weight * source[pl.ds(block * 8, 8), :]
        if cells % 8:
            at = pl.ds(whole * 32 + s, cells % 8, stride=4)
            total[at, :] = (
                total[at, :]
                + weight[: cells % 8] * source[pl.ds(whole * 8, cells % 8), :]
            )

    @pl.when(has_up)
    def _():
        to_down.wait_recv()
        add_span(from_up, 3)

    @pl.when(has_down)
    def _():
        to_up.wait_recv()
        add_span(from_down, 0)

    pltpu.make_async_copy(ghost, ghost, recv_sem.at[5]).wait()
    for n in range(planes):
        at = pl.ds(16 * n + 12, 4)
        total[at, :] = total[at, :] + 0.1 * ghost[n]

    pltpu.make_async_copy(ghost, ghost, send_sem.at[0]).wait()
    to_right.wait_send()
    to_left.wait_send()

    @pl.when(has_up)
    def _():
        to_up.wait_send()

    @pl.when(has_down)
    def _():
        to_down.wait_send()

    @pl.when(is_home)
    def _():
        others = turned.at[pl.ds(0, sectors - 1)]
        pltpu.make_async_copy(others, others, send_sem.at[5]).wait()


def solution(mesh):
    sectors, slabs = mesh.shape["sec"], mesh.shape["span"]

    def on_device(state, viscosity, jacobian, frequency, offsets):
        _, times, fields, axial, span, lanes = state.shape
        planes = times * fields
        share = planes // (sectors - len(AWAY))
        rows = planes * axial * span
        edge = pltpu.VMEM((planes * axial, lanes), jnp.float32)
        pairs = pltpu.VMEM((16, lanes), jnp.float32)
        anywhere = pl.BlockSpec(memory_space=pltpu.HBM)
        out = pl.pallas_call(
            functools.partial(kernel, sectors, slabs, times, fields, share, AWAY),
            out_shape=pltpu.VMEM((rows, lanes), jnp.float32),
            in_specs=[anywhere] * 6,
            out_specs=pl.BlockSpec(memory_space=pltpu.VMEM),
            scratch_shapes=[
                pltpu.VMEM((rows, lanes), jnp.float32),
                pltpu.VMEM((16, lanes), jnp.float32),
                pltpu.SMEM((fields, 1, fields), jnp.float32),
                pltpu.SMEM((1,), jnp.float32),
                pltpu.SMEM((times,), jnp.int32),
                edge, edge, edge, edge,
                pairs, pairs, pairs,
                pltpu.VMEM((sectors, share, span, lanes), jnp.float32),
                pltpu.VMEM((sectors, share, span, lanes), jnp.float32),
                pltpu.VMEM((planes, span, lanes), jnp.float32),
                pltpu.SemaphoreType.DMA((5,)),
                pltpu.SemaphoreType.DMA((6,)),
                pltpu.SemaphoreType.DMA((6,)),
                pltpu.SemaphoreType.REGULAR((4,)),
                pltpu.SemaphoreType.REGULAR((2,)),
            ],
            compiler_params=pltpu.CompilerParams(collective_id=0, has_side_effects=True),
        )(
            state.reshape(planes, axial, span, lanes),
            state.reshape(rows, lanes),
            viscosity.reshape(axial * span, lanes),
            jacobian.reshape(fields, 1, fields),
            frequency,
            offsets,
        )
        return out.reshape(state.shape)

    return jax.shard_map(
        on_device,
        mesh=mesh,
        in_specs=(
            P("row", None, None, None, "span", "sec"),
            P("row", None, "span", "sec"),
            P("row", None, None),
            P("row"),
            P(),
        ),
        out_specs=P("row", None, None, None, "span", "sec"),
        check_vma=False,
    )
```

```python
import functools
import math

import jax
import jax.numpy as jnp
from jax import lax
from jax.experimental import pallas as pl
from jax.experimental.pallas import tpu as pltpu
from jax.sharding import PartitionSpec as P

MESH = pl.DeviceIdType.MESH
LANES = 128
DEPTHS = 4
AWAY = (0, 12, 20)


def kernel(
    sectors, slabs, times, fields, share, away,
    strip_src, state_src, visc_src, jac_src, freq_src, offs_src, total,
    state, strip, coeff, jac, freq, offs,
    edge_up, edge_down, from_up, from_down,
    edges, edges_left, edges_right,
    gathered, turned, ghost,
    load_sem, send_sem, recv_sem, ready_sem, home_sem,
):
    row = lax.axis_index("row")
    me = lax.axis_index("sec")
    slab = lax.axis_index("span")
    planes = times * fields
    cells = planes * 4
    annulus = sectors * LANES

    def is_holder(sector):
        held = sector != away[0]
        for other in away[1:]:
            held = held & (sector != other)
        return held

    def rank(sector):
        before = sector
        for other in away:
            before = before - jnp.where(sector > other, 1, 0)
        return before

    is_home = is_holder(me)
    mine = rank(me)

    depth = lax.rem(slab, DEPTHS)
    ordered = depth == DEPTHS - 1
    is_root = (row == 0) & (me == 0) & (slab == 0)

    def lateness(at_row, sector):
        along = sector & 7
        late = 10 * jnp.minimum(along, 8 - along) + jnp.where(along > 3, 10, 0) + 60 * (sector >> 3)
        return late * (2 * sectors) + 2 * sector + at_row

    here = lateness(row, me)

    def root_at(at_row, sector):
        return (at_row == 0) & (sector == 0) & (slab == 0)

    targets = [lax.rem(me + step, sectors) for step in range(sectors)]
    held = [is_holder(target) for target in targets]
    far_first = sorted(range(sectors), key=lambda step: -min(step % 8, 8 - step % 8))

    def choose(one, other):
        return (ordered & one) | (~ordered & other)

    across_later = [ordered & (lateness(1 - row, target) > here) for target in targets]
    along_later = [lateness(row, target) > here for target in targets]
    across_greet = [choose(later, is_home) for later in across_later]
    across_wait = [choose(~later, at) for later, at in zip(across_later, held)]
    along_greet, along_wait, along_tell, along_miss = [None], [None], [None], [None]
    for step in range(1, sectors):
        later, at = along_later[step], held[step]
        greet, wait = is_home & ~at, ~is_home & at
        if step in (1, sectors - 1):
            greet, wait = greet | ~is_root, wait | ~root_at(row, targets[step])
        along_greet.append(choose(later, greet))
        along_wait.append(choose(~later, wait))
        along_tell.append(choose(~later & at, ~is_home & at))
        along_miss.append(choose(later, is_home & ~at))

    has_up = slab < slabs - 1
    has_down = slab > 0
    up_later = has_up & (depth != DEPTHS - 1) & ~is_root
    up_earlier = has_up & ~up_later
    down_later = has_down & ((depth == 0) | ((row == 0) & (me == 0) & (slab == 1)))
    down_earlier = has_down & ~down_later

    def beside(step):
        root, later = root_at(row, targets[step]), along_later[step]
        return choose(~later, ~root), choose(~later, is_root), choose(later, root)

    neighbours = (
        (up_earlier, up_earlier, up_later, {"span": slab + 1}, 0, 1),
        (down_earlier, down_earlier, down_later, {"span": slab - 1}, 1, 0),
        (*beside(1), {"sec": targets[1]}, 2, 3),
        (*beside(sectors - 1), {"sec": targets[sectors - 1]}, 3, 2),
    )

    barrier = pltpu.get_barrier_semaphore()

    def signal(sem, device):
        pl.semaphore_signal(sem, inc=1, device_id=device, device_id_type=MESH)

    def count(flags):
        return sum(flag.astype(jnp.int32) for flag in flags)

    for step in far_first:
        pl.when(across_greet[step])(
            functools.partial(signal, barrier, {"row": 1 - row, "sec": targets[step]})
        )
    for step in far_first:
        if step:
            pl.when(along_greet[step])(
                functools.partial(signal, barrier, {"sec": targets[step]})
            )
    for _, _, later, device, _, _ in neighbours[:2]:
        pl.when(later)(functools.partial(signal, barrier, device))

    planes_load = pltpu.make_async_copy(strip_src.at[:, 3], strip, load_sem.at[5])
    planes_load.start()
    loads = (
        pltpu.make_async_copy(state_src, state, load_sem.at[0]),
        pltpu.make_async_copy(visc_src, coeff, load_sem.at[1]),
        pltpu.make_async_copy(jac_src, jac, load_sem.at[2]),
        pltpu.make_async_copy(freq_src, freq, load_sem.at[3]),
        pltpu.make_async_copy(offs_src, offs, load_sem.at[4]),
    )
    for load in loads:
        load.start()

    pl.semaphore_wait(
        barrier, count(across_wait + along_wait[1:] + [up_earlier, down_earlier])
    )
    planes_load.wait()
    for _, told, _, device, _, there in neighbours:
        pl.when(told)(functools.partial(signal, ready_sem.at[there], device))

    def spread(chosen):
        for step in far_first:

            @pl.when(held[step] & chosen[step])
            def _(target=targets[step]):
                pltpu.make_async_remote_copy(
                    src_ref=strip.at[pl.ds(share * rank(target), share)],
                    dst_ref=gathered.at[me],
                    send_sem=send_sem.at[0],
                    recv_sem=recv_sem.at[0],
                    device_id={"row": 1 - row, "sec": target},
                    device_id_type=MESH,
                ).start()

    @pl.when(is_home & ordered)
    def _():
        for step in far_first:
            pl.when(~across_later[step])(
                functools.partial(
                    signal, home_sem.at[0], {"row": 1 - row, "sec": targets[step]}
                )
            )

    spread([~later for later in across_later])
    for step in range(1, sectors):
        pl.when(along_tell[step])(
            functools.partial(signal, home_sem.at[1], {"sec": targets[step]})
        )

    for load in loads:
        load.wait()

    edge_up[...] = state[pl.ds(3, cells, stride=4), :]
    edge_down[...] = state[pl.ds(0, cells, stride=4), :]
    to_right = pltpu.make_async_remote_copy(
        src_ref=edges, dst_ref=edges_left, send_sem=send_sem.at[1], recv_sem=recv_sem.at[1],
        device_id={"sec": targets[1]}, device_id_type=MESH,
    )
    to_left = pltpu.make_async_remote_copy(
        src_ref=edges, dst_ref=edges_right, send_sem=send_sem.at[2], recv_sem=recv_sem.at[2],
        device_id={"sec": targets[sectors - 1]}, device_id_type=MESH,
    )
    to_up = pltpu.make_async_remote_copy(
        src_ref=edge_up, dst_ref=from_down, send_sem=send_sem.at[3], recv_sem=recv_sem.at[3],
        device_id={"span": slab + 1}, device_id_type=MESH,
    )
    to_down = pltpu.make_async_remote_copy(
        src_ref=edge_down, dst_ref=from_up, send_sem=send_sem.at[4], recv_sem=recv_sem.at[4],
        device_id={"span": slab - 1}, device_id_type=MESH,
    )
    halos = tuple(zip((to_up, to_down, to_right, to_left), neighbours))
    for halo, (earlier, _, _, _, _, _) in halos[:2]:
        pl.when(earlier)(halo.start)

    lane = lax.broadcasted_iota(jnp.int32, (8, LANES), 1)
    sub = lax.broadcasted_iota(jnp.int32, (8, LANES), 0)

    def rows_of(t, f, half):
        return pl.ds(pl.multiple_of(t * (fields * 16) + (f * 16 + half * 8), 8), 8)

    def pack(t, held):
        packed = []
        for half in range(2):
            part = jnp.zeros((8, LANES), jnp.float32)
            for f in range(fields):
                turn = pltpu.roll(state[rows_of(t, f, half), :], 2 * f + 1, 1)
                part = jnp.where((lane >> 1) == f, turn, part)
            packed.append(held[half] + pltpu.roll(part, t * (2 * fields), 1))
        return tuple(packed)

    zero = jnp.zeros((8, LANES), jnp.float32)
    packed = lax.fori_loop(0, times, pack, (zero, zero))
    edges[pl.ds(0, 8), :] = packed[0]
    edges[pl.ds(8, 8), :] = packed[1]

    for halo, (earlier, _, _, _, _, _) in halos[2:]:
        pl.when(earlier)(halo.start)

    weights = [
        freq[0] * jnp.float32(-0.05 * (-1.0) ** m / math.sin(math.pi * m / times))
        for m in range(1, times // 2 + 1)
    ]

    @pl.loop(0, fields)
    def _(f):
        for half in range(2):
            at = [
                pl.ds(pl.multiple_of(f * 16 + (t * fields * 16 + half * 8), 8), 8)
                for t in range(times)
            ]
            values = [state[at[t], :] for t in range(times)]
            for t in range(times):
                acc = None
                for m, weight in enumerate(weights, 1):
                    term = weight * (values[(t - m) % times] - values[(t + m) % times])
                    acc = term if acc is None else acc + term
                total[at[t], :] = acc

    def send_later(index, now):
        halo, (_, _, later, _, told, _) = halos[index]

        @pl.when(later & now)
        def _():
            pl.semaphore_wait(ready_sem.at[told], 1)
            halo.start()

    across = count([later & at for later, at in zip(across_later, held)])

    @pl.when(across > 0)
    def _():
        pl.semaphore_wait(home_sem.at[0], across)
        spread(across_later)

    beside_root = (row == 0) & (slab == 0)
    root_right = beside_root & (targets[1] == 0)
    root_left = beside_root & (targets[sectors - 1] == 0)
    send_later(2, ~root_right)
    send_later(3, ~root_left)
    soon = (depth == DEPTHS - 2) | (depth == DEPTHS - 3)
    send_later(0, soon)

    @pl.when(is_home)
    def _():
        pltpu.make_async_copy(gathered, gathered, recv_sem.at[0]).wait()
        along = count(along_miss[1:])

        @pl.when(along > 0)
        def _():
            pl.semaphore_wait(home_sem.at[1], along)

        thin = lax.broadcasted_iota(jnp.int32, (4, LANES), 1)
        wholes, rests = [], []
        for part in range(share):
            offset = offs[(share * mine + part) // fields]
            shift = jnp.where(row == 0, offset, annulus - offset)
            wholes.append(shift >> 7)
            rests.append(shift & (LANES - 1))

        def source(sector, part):
            at = lax.rem(sector + (2 * sectors - wholes[part]), sectors)
            return pltpu.roll(gathered[at, part], rests[part], 1)

        before = [source(me - 1, part) for part in range(share)]
        there = ghost.at[pl.ds(share * mine, share)]
        for step in range(sectors):
            target = lax.rem(me + step, sectors)
            for part in range(share):
                after = source(me + step, part)
                turned[target, part] = jnp.where(thin >= rests[part], after, before[part])
                before[part] = after
            if step == 0:
                pltpu.make_async_copy(turned.at[me], there, recv_sem.at[5]).start()
            else:
                pltpu.make_async_remote_copy(
                    src_ref=turned.at[target],
                    dst_ref=there,
                    send_sem=send_sem.at[5],
                    recv_sem=recv_sem.at[5],
                    device_id={"sec": target},
                    device_id_type=MESH,
                ).start()

    send_later(2, root_right)
    send_later(3, root_left)
    send_later(1, has_down)
    send_later(0, ~soon)

    to_right.wait_recv()
    to_left.wait_recv()
    mix = [[jac[f, 0, g] * jnp.float32(-0.05) for g in range(fields)] for f in range(fields)]
    diffuse = [coeff[pl.ds(8 * half, 8), :] * jnp.float32(0.1) for half in range(2)]
    first_span = (sub & 3) == 0
    last_span = (sub & 3) == 3
    low = sub < 4

    @pl.loop(0, times)
    def _(t):
        turn = lax.rem(LANES - t * (2 * fields), LANES)
        lefts = [pltpu.roll(edges_left[pl.ds(8 * h, 8), :], turn, 1) for h in range(2)]
        rights = [pltpu.roll(edges_right[pl.ds(8 * h, 8), :], turn, 1) for h in range(2)]
        slopes = []
        for f in range(fields):
            pair = [state[rows_of(t, f, half), :] for half in range(2)]
            swapped = [pltpu.roll(v, 4, 0) for v in pair]
            middle = jnp.where(low, swapped[0], swapped[1])
            axial = (
                middle + jnp.where(low, 0.0, swapped[0]),
                middle + jnp.where(low, swapped[1], 0.0),
            )
            slope = []
            for half in range(2):
                v = pair[half]
                plus = jnp.where(
                    lane == LANES - 1,
                    pltpu.roll(rights[half], (LANES - 2 - 2 * f) % LANES, 1),
                    pltpu.roll(v, LANES - 1, 1),
                )
                minus = jnp.where(
                    lane == 0,
                    pltpu.roll(lefts[half], (LANES - 2 * f) % LANES, 1),
                    pltpu.roll(v, 1, 1),
                )
                around = plus + minus
                slope.append(plus - minus)
                around = around + jnp.where(last_span, 0.0, pltpu.roll(v, 7, 0))
                around = around + jnp.where(first_span, 0.0, pltpu.roll(v, 1, 0))
                at = rows_of(t, f, half)
                total[at, :] = (
                    total[at, :]
                    + 0.8 * v
                    + 0.1 * axial[half]
                    + diffuse[half] * (around - 4.0 * v)
                )
            slopes.append(slope)
        for f in range(fields):
            for half in range(2):
                acc = mix[f][0] * slopes[0][half]
                for g in range(1, fields):
                    acc = acc + mix[f][g] * slopes[g][half]
                at = rows_of(t, f, half)
                total[at, :] = total[at, :] + acc

    def span_weights(s):
        rows = [coeff[pl.ds(4 * a + s, 1), :] * jnp.float32(0.1) for a in range(4)]
        out = jnp.broadcast_to(rows[3], (8, LANES))
        for a in range(3):
            out = jnp.where((sub & 3) == a, jnp.broadcast_to(rows[a], (8, LANES)), out)
        return out

    def add_span(source, s):
        weight = span_weights(s)
        whole = cells // 8
        for block in range(whole):
            at = pl.ds(block * 32 + s, 8, stride=4)
            total[at, :] = total[at, :] + weight * source[pl.ds(block * 8, 8), :]
        if cells % 8:
            at = pl.ds(whole * 32 + s, cells % 8, stride=4)
            total[at, :] = (
                total[at, :]
                + weight[: cells % 8] * source[pl.ds(whole * 8, cells % 8), :]
            )

    @pl.when(has_up)
    def _():
        to_down.wait_recv()
        add_span(from_up, 3)

    @pl.when(has_down)
    def _():
        to_up.wait_recv()
        add_span(from_down, 0)

    pltpu.make_async_copy(ghost, ghost, recv_sem.at[5]).wait()
    for n in range(planes):
        at = pl.ds(16 * n + 12, 4)
        total[at, :] = total[at, :] + 0.1 * ghost[n]

    pltpu.make_async_copy(ghost, ghost, send_sem.at[0]).wait()
    to_right.wait_send()
    to_left.wait_send()

    @pl.when(has_up)
    def _():
        to_up.wait_send()

    @pl.when(has_down)
    def _():
        to_down.wait_send()

    @pl.when(is_home)
    def _():
        others = turned.at[pl.ds(0, sectors - 1)]
        pltpu.make_async_copy(others, others, send_sem.at[5]).wait()


def solution(mesh):
    sectors, slabs = mesh.shape["sec"], mesh.shape["span"]

    def on_device(state, viscosity, jacobian, frequency, offsets):
        _, times, fields, axial, span, lanes = state.shape
        planes = times * fields
        share = planes // (sectors - len(AWAY))
        rows = planes * axial * span
        edge = pltpu.VMEM((planes * axial, lanes), jnp.float32)
        pairs = pltpu.VMEM((16, lanes), jnp.float32)
        anywhere = pl.BlockSpec(memory_space=pltpu.HBM)
        out = pl.pallas_call(
            functools.partial(kernel, sectors, slabs, times, fields, share, AWAY),
            out_shape=pltpu.VMEM((rows, lanes), jnp.float32),
            in_specs=[anywhere] * 6,
            out_specs=pl.BlockSpec(memory_space=pltpu.VMEM),
            scratch_shapes=[
                pltpu.VMEM((rows, lanes), jnp.float32),
                pltpu.VMEM((planes, span, lanes), jnp.float32),
                pltpu.VMEM((16, lanes), jnp.float32),
                pltpu.SMEM((fields, 1, fields), jnp.float32),
                pltpu.SMEM((1,), jnp.float32),
                pltpu.SMEM((times,), jnp.int32),
                edge, edge, edge, edge,
                pairs, pairs, pairs,
                pltpu.VMEM((sectors, share, span, lanes), jnp.float32),
                pltpu.VMEM((sectors, share, span, lanes), jnp.float32),
                pltpu.VMEM((planes, span, lanes), jnp.float32),
                pltpu.SemaphoreType.DMA((6,)),
                pltpu.SemaphoreType.DMA((6,)),
                pltpu.SemaphoreType.DMA((6,)),
                pltpu.SemaphoreType.REGULAR((4,)),
                pltpu.SemaphoreType.REGULAR((2,)),
            ],
            compiler_params=pltpu.CompilerParams(collective_id=0, has_side_effects=True),
        )(
            state.reshape(planes, axial, span, lanes),
            state.reshape(rows, lanes),
            viscosity.reshape(axial * span, lanes),
            jacobian.reshape(fields, 1, fields),
            frequency,
            offsets,
        )
        return out.reshape(state.shape)

    return jax.shard_map(
        on_device,
        mesh=mesh,
        in_specs=(
            P("row", None, None, None, "span", "sec"),
            P("row", None, "span", "sec"),
            P("row", None, None),
            P("row"),
            P(),
        ),
        out_specs=P("row", None, None, None, "span", "sec"),
        check_vma=False,
    )
```

```python
import functools
import math

import jax
import jax.numpy as jnp
from jax import lax
from jax.experimental import pallas as pl
from jax.experimental.pallas import tpu as pltpu
from jax.sharding import PartitionSpec as P

MESH = pl.DeviceIdType.MESH
LANES = 128
DEPTHS = 4
AWAY = (0, 20, 21)


def kernel(
    sectors, slabs, times, fields, share, away,
    strip_src, state_src, visc_src, jac_src, freq_src, offs_src, total,
    state, strip, coeff, jac, freq, offs,
    edge_up, edge_down, from_up, from_down,
    edges, edges_left, edges_right,
    gathered, turned, ghost,
    load_sem, send_sem, recv_sem, ready_sem, home_sem,
):
    row = lax.axis_index("row")
    me = lax.axis_index("sec")
    slab = lax.axis_index("span")
    planes = times * fields
    cells = planes * 4
    annulus = sectors * LANES

    def is_holder(sector):
        held = sector != away[0]
        for other in away[1:]:
            held = held & (sector != other)
        return held

    def rank(sector):
        before = sector
        for other in away:
            before = before - jnp.where(sector > other, 1, 0)
        return before

    is_home = is_holder(me)
    mine = rank(me)

    depth = lax.rem(slab, DEPTHS)
    ordered = depth == DEPTHS - 1
    is_root = (row == 0) & (me == 0) & (slab == 0)

    def lateness(at_row, sector):
        along = sector & 7
        late = 10 * jnp.minimum(along, 8 - along) + jnp.where(along > 3, 10, 0) + 60 * (sector >> 3)
        return late * (2 * sectors) + 2 * sector + at_row

    here = lateness(row, me)

    def root_at(at_row, sector):
        return (at_row == 0) & (sector == 0) & (slab == 0)

    targets = [lax.rem(me + step, sectors) for step in range(sectors)]
    held = [is_holder(target) for target in targets]
    far_first = sorted(range(sectors), key=lambda step: -min(step % 8, 8 - step % 8))

    def choose(one, other):
        return (ordered & one) | (~ordered & other)

    across_later = [ordered & (lateness(1 - row, target) > here) for target in targets]
    along_later = [lateness(row, target) > here for target in targets]
    across_greet = [choose(later, is_home) for later in across_later]
    across_wait = [choose(~later, at) for later, at in zip(across_later, held)]
    along_greet, along_wait, along_tell, along_miss = [None], [None], [None], [None]
    for step in range(1, sectors):
        later, at = along_later[step], held[step]
        greet, wait = is_home & ~at, ~is_home & at
        if step in (1, sectors - 1):
            greet, wait = greet | ~is_root, wait | ~root_at(row, targets[step])
        along_greet.append(choose(later, greet))
        along_wait.append(choose(~later, wait))
        along_tell.append(choose(~later & at, ~is_home & at))
        along_miss.append(choose(later, is_home & ~at))

    has_up = slab < slabs - 1
    has_down = slab > 0
    up_later = has_up & (depth != DEPTHS - 1) & ~is_root
    up_earlier = has_up & ~up_later
    down_later = has_down & ((depth == 0) | ((row == 0) & (me == 0) & (slab == 1)))
    down_earlier = has_down & ~down_later

    def beside(step):
        root, later = root_at(row, targets[step]), along_later[step]
        return choose(~later, ~root), choose(~later, is_root), choose(later, root)

    neighbours = (
        (up_earlier, up_earlier, up_later, {"span": slab + 1}, 0, 1),
        (down_earlier, down_earlier, down_later, {"span": slab - 1}, 1, 0),
        (*beside(1), {"sec": targets[1]}, 2, 3),
        (*beside(sectors - 1), {"sec": targets[sectors - 1]}, 3, 2),
    )

    barrier = pltpu.get_barrier_semaphore()

    def signal(sem, device):
        pl.semaphore_signal(sem, inc=1, device_id=device, device_id_type=MESH)

    def count(flags):
        return sum(flag.astype(jnp.int32) for flag in flags)

    for step in far_first:
        pl.when(across_greet[step])(
            functools.partial(signal, barrier, {"row": 1 - row, "sec": targets[step]})
        )
    for step in far_first:
        if step:
            pl.when(along_greet[step])(
                functools.partial(signal, barrier, {"sec": targets[step]})
            )
    for _, _, later, device, _, _ in neighbours[:2]:
        pl.when(later)(functools.partial(signal, barrier, device))

    planes_load = pltpu.make_async_copy(strip_src.at[:, 3], strip, load_sem.at[5])
    planes_load.start()
    loads = (
        pltpu.make_async_copy(state_src, state, load_sem.at[0]),
        pltpu.make_async_copy(visc_src, coeff, load_sem.at[1]),
        pltpu.make_async_copy(jac_src, jac, load_sem.at[2]),
        pltpu.make_async_copy(freq_src, freq, load_sem.at[3]),
        pltpu.make_async_copy(offs_src, offs, load_sem.at[4]),
    )
    for load in loads:
        load.start()

    pl.semaphore_wait(
        barrier, count(across_wait + along_wait[1:] + [up_earlier, down_earlier])
    )
    planes_load.wait()
    for _, told, _, device, _, there in neighbours:
        pl.when(told)(functools.partial(signal, ready_sem.at[there], device))

    def spread(chosen):
        for step in far_first:

            @pl.when(held[step] & chosen[step])
            def _(target=targets[step]):
                pltpu.make_async_remote_copy(
                    src_ref=strip.at[pl.ds(share * rank(target), share)],
                    dst_ref=gathered.at[me],
                    send_sem=send_sem.at[0],
                    recv_sem=recv_sem.at[0],
                    device_id={"row": 1 - row, "sec": target},
                    device_id_type=MESH,
                ).start()

    @pl.when(is_home & ordered)
    def _():
        for step in far_first:
            pl.when(~across_later[step])(
                functools.partial(
                    signal, home_sem.at[0], {"row": 1 - row, "sec": targets[step]}
                )
            )

    spread([~later for later in across_later])
    for step in range(1, sectors):
        pl.when(along_tell[step])(
            functools.partial(signal, home_sem.at[1], {"sec": targets[step]})
        )

    for load in loads:
        load.wait()

    edge_up[...] = state[pl.ds(3, cells, stride=4), :]
    edge_down[...] = state[pl.ds(0, cells, stride=4), :]
    to_right = pltpu.make_async_remote_copy(
        src_ref=edges, dst_ref=edges_left, send_sem=send_sem.at[1], recv_sem=recv_sem.at[1],
        device_id={"sec": targets[1]}, device_id_type=MESH,
    )
    to_left = pltpu.make_async_remote_copy(
        src_ref=edges, dst_ref=edges_right, send_sem=send_sem.at[2], recv_sem=recv_sem.at[2],
        device_id={"sec": targets[sectors - 1]}, device_id_type=MESH,
    )
    to_up = pltpu.make_async_remote_copy(
        src_ref=edge_up, dst_ref=from_down, send_sem=send_sem.at[3], recv_sem=recv_sem.at[3],
        device_id={"span": slab + 1}, device_id_type=MESH,
    )
    to_down = pltpu.make_async_remote_copy(
        src_ref=edge_down, dst_ref=from_up, send_sem=send_sem.at[4], recv_sem=recv_sem.at[4],
        device_id={"span": slab - 1}, device_id_type=MESH,
    )
    halos = tuple(zip((to_up, to_down, to_right, to_left), neighbours))
    for halo, (earlier, _, _, _, _, _) in halos[:2]:
        pl.when(earlier)(halo.start)

    lane = lax.broadcasted_iota(jnp.int32, (8, LANES), 1)
    sub = lax.broadcasted_iota(jnp.int32, (8, LANES), 0)

    def rows_of(t, f, half):
        return pl.ds(pl.multiple_of(t * (fields * 16) + (f * 16 + half * 8), 8), 8)

    def pack(t, held):
        packed = []
        for half in range(2):
            part = jnp.zeros((8, LANES), jnp.float32)
            for f in range(fields):
                turn = pltpu.roll(state[rows_of(t, f, half), :], 2 * f + 1, 1)
                part = jnp.where((lane >> 1) == f, turn, part)
            packed.append(held[half] + pltpu.roll(part, t * (2 * fields), 1))
        return tuple(packed)

    zero = jnp.zeros((8, LANES), jnp.float32)
    packed = lax.fori_loop(0, times, pack, (zero, zero))
    edges[pl.ds(0, 8), :] = packed[0]
    edges[pl.ds(8, 8), :] = packed[1]

    for halo, (earlier, _, _, _, _, _) in halos[2:]:
        pl.when(earlier)(halo.start)

    weights = [
        freq[0] * jnp.float32(-0.05 * (-1.0) ** m / math.sin(math.pi * m / times))
        for m in range(1, times // 2 + 1)
    ]

    @pl.loop(0, fields)
    def _(f):
        for half in range(2):
            at = [
                pl.ds(pl.multiple_of(f * 16 + (t * fields * 16 + half * 8), 8), 8)
                for t in range(times)
            ]
            values = [state[at[t], :] for t in range(times)]
            for t in range(times):
                acc = None
                for m, weight in enumerate(weights, 1):
                    term = weight * (values[(t - m) % times] - values[(t + m) % times])
                    acc = term if acc is None else acc + term
                total[at[t], :] = acc

    def send_later(index, now):
        halo, (_, _, later, _, told, _) = halos[index]

        @pl.when(later & now)
        def _():
            pl.semaphore_wait(ready_sem.at[told], 1)
            halo.start()

    across = count([later & at for later, at in zip(across_later, held)])

    @pl.when(across > 0)
    def _():
        pl.semaphore_wait(home_sem.at[0], across)
        spread(across_later)

    beside_root = (row == 0) & (slab == 0)
    root_right = beside_root & (targets[1] == 0)
    root_left = beside_root & (targets[sectors - 1] == 0)
    send_later(2, ~root_right)
    send_later(3, ~root_left)
    soon = depth == DEPTHS - 2
    send_later(0, soon)

    @pl.when(is_home)
    def _():
        pltpu.make_async_copy(gathered, gathered, recv_sem.at[0]).wait()
        along = count(along_miss[1:])

        @pl.when(along > 0)
        def _():
            pl.semaphore_wait(home_sem.at[1], along)

        thin = lax.broadcasted_iota(jnp.int32, (4, LANES), 1)
        wholes, rests = [], []
        for part in range(share):
            offset = offs[(share * mine + part) // fields]
            shift = jnp.where(row == 0, offset, annulus - offset)
            wholes.append(shift >> 7)
            rests.append(shift & (LANES - 1))

        def source(sector, part):
            at = lax.rem(sector + (2 * sectors - wholes[part]), sectors)
            return pltpu.roll(gathered[at, part], rests[part], 1)

        before = [source(me - 1, part) for part in range(share)]
        there = ghost.at[pl.ds(share * mine, share)]
        for step in range(sectors):
            target = lax.rem(me + step, sectors)
            for part in range(share):
                after = source(me + step, part)
                turned[target, part] = jnp.where(thin >= rests[part], after, before[part])
                before[part] = after
        pltpu.make_async_copy(turned.at[me], there, recv_sem.at[5]).start()
        for step in far_first:
            if step:
                pltpu.make_async_remote_copy(
                    src_ref=turned.at[targets[step]],
                    dst_ref=there,
                    send_sem=send_sem.at[5],
                    recv_sem=recv_sem.at[5],
                    device_id={"sec": targets[step]},
                    device_id_type=MESH,
                ).start()

    send_later(2, root_right)
    send_later(3, root_left)
    send_later(1, has_down)
    send_later(0, ~soon)

    to_right.wait_recv()
    to_left.wait_recv()
    mix = [[jac[f, 0, g] * jnp.float32(-0.05) for g in range(fields)] for f in range(fields)]
    diffuse = [coeff[pl.ds(8 * half, 8), :] * jnp.float32(0.1) for half in range(2)]
    first_span = (sub & 3) == 0
    last_span = (sub & 3) == 3
    low = sub < 4

    @pl.loop(0, times)
    def _(t):
        turn = lax.rem(LANES - t * (2 * fields), LANES)
        lefts = [pltpu.roll(edges_left[pl.ds(8 * h, 8), :], turn, 1) for h in range(2)]
        rights = [pltpu.roll(edges_right[pl.ds(8 * h, 8), :], turn, 1) for h in range(2)]
        slopes = []
        for f in range(fields):
            pair = [state[rows_of(t, f, half), :] for half in range(2)]
            swapped = [pltpu.roll(v, 4, 0) for v in pair]
            middle = jnp.where(low, swapped[0], swapped[1])
            axial = (
                middle + jnp.where(low, 0.0, swapped[0]),
                middle + jnp.where(low, swapped[1], 0.0),
            )
            slope = []
            for half in range(2):
                v = pair[half]
                plus = jnp.where(
                    lane == LANES - 1,
                    pltpu.roll(rights[half], (LANES - 2 - 2 * f) % LANES, 1),
                    pltpu.roll(v, LANES - 1, 1),
                )
                minus = jnp.where(
                    lane == 0,
                    pltpu.roll(lefts[half], (LANES - 2 * f) % LANES, 1),
                    pltpu.roll(v, 1, 1),
                )
                around = plus + minus
                slope.append(plus - minus)
                around = around + jnp.where(last_span, 0.0, pltpu.roll(v, 7, 0))
                around = around + jnp.where(first_span, 0.0, pltpu.roll(v, 1, 0))
                at = rows_of(t, f, half)
                total[at, :] = (
                    total[at, :]
                    + 0.8 * v
                    + 0.1 * axial[half]
                    + diffuse[half] * (around - 4.0 * v)
                )
            slopes.append(slope)
        for f in range(fields):
            for half in range(2):
                acc = mix[f][0] * slopes[0][half]
                for g in range(1, fields):
                    acc = acc + mix[f][g] * slopes[g][half]
                at = rows_of(t, f, half)
                total[at, :] = total[at, :] + acc

    def span_weights(s):
        rows = [coeff[pl.ds(4 * a + s, 1), :] * jnp.float32(0.1) for a in range(4)]
        out = jnp.broadcast_to(rows[3], (8, LANES))
        for a in range(3):
            out = jnp.where((sub & 3) == a, jnp.broadcast_to(rows[a], (8, LANES)), out)
        return out

    def add_span(source, s):
        weight = span_weights(s)
        whole = cells // 8
        for block in range(whole):
            at = pl.ds(block * 32 + s, 8, stride=4)
            total[at, :] = total[at, :] + weight * source[pl.ds(block * 8, 8), :]
        if cells % 8:
            at = pl.ds(whole * 32 + s, cells % 8, stride=4)
            total[at, :] = (
                total[at, :]
                + weight[: cells % 8] * source[pl.ds(whole * 8, cells % 8), :]
            )

    @pl.when(has_up)
    def _():
        to_down.wait_recv()
        add_span(from_up, 3)

    @pl.when(has_down)
    def _():
        to_up.wait_recv()
        add_span(from_down, 0)

    pltpu.make_async_copy(ghost, ghost, recv_sem.at[5]).wait()
    for n in range(planes):
        at = pl.ds(16 * n + 12, 4)
        total[at, :] = total[at, :] + 0.1 * ghost[n]

    pltpu.make_async_copy(ghost, ghost, send_sem.at[0]).wait()
    to_right.wait_send()
    to_left.wait_send()

    @pl.when(has_up)
    def _():
        to_up.wait_send()

    @pl.when(has_down)
    def _():
        to_down.wait_send()

    @pl.when(is_home)
    def _():
        others = turned.at[pl.ds(0, sectors - 1)]
        pltpu.make_async_copy(others, others, send_sem.at[5]).wait()


def solution(mesh):
    sectors, slabs = mesh.shape["sec"], mesh.shape["span"]

    def on_device(state, viscosity, jacobian, frequency, offsets):
        _, times, fields, axial, span, lanes = state.shape
        planes = times * fields
        share = planes // (sectors - len(AWAY))
        rows = planes * axial * span
        edge = pltpu.VMEM((planes * axial, lanes), jnp.float32)
        pairs = pltpu.VMEM((16, lanes), jnp.float32)
        anywhere = pl.BlockSpec(memory_space=pltpu.HBM)
        out = pl.pallas_call(
            functools.partial(kernel, sectors, slabs, times, fields, share, AWAY),
            out_shape=pltpu.VMEM((rows, lanes), jnp.float32),
            in_specs=[anywhere] * 6,
            out_specs=pl.BlockSpec(memory_space=pltpu.VMEM),
            scratch_shapes=[
                pltpu.VMEM((rows, lanes), jnp.float32),
                pltpu.VMEM((planes, span, lanes), jnp.float32),
                pltpu.VMEM((16, lanes), jnp.float32),
                pltpu.SMEM((fields, 1, fields), jnp.float32),
                pltpu.SMEM((1,), jnp.float32),
                pltpu.SMEM((times,), jnp.int32),
                edge, edge, edge, edge,
                pairs, pairs, pairs,
                pltpu.VMEM((sectors, share, span, lanes), jnp.float32),
                pltpu.VMEM((sectors, share, span, lanes), jnp.float32),
                pltpu.VMEM((planes, span, lanes), jnp.float32),
                pltpu.SemaphoreType.DMA((6,)),
                pltpu.SemaphoreType.DMA((6,)),
                pltpu.SemaphoreType.DMA((6,)),
                pltpu.SemaphoreType.REGULAR((4,)),
                pltpu.SemaphoreType.REGULAR((2,)),
            ],
            compiler_params=pltpu.CompilerParams(collective_id=0, has_side_effects=True),
        )(
            state.reshape(planes, axial, span, lanes),
            state.reshape(rows, lanes),
            viscosity.reshape(axial * span, lanes),
            jacobian.reshape(fields, 1, fields),
            frequency,
            offsets,
        )
        return out.reshape(state.shape)

    return jax.shard_map(
        on_device,
        mesh=mesh,
        in_specs=(
            P("row", None, None, None, "span", "sec"),
            P("row", None, "span", "sec"),
            P("row", None, None),
            P("row"),
            P(),
        ),
        out_specs=P("row", None, None, None, "span", "sec"),
        check_vma=False,
    )
```

```python
import functools
import math

import jax
import jax.numpy as jnp
from jax import lax
from jax.experimental import pallas as pl
from jax.experimental.pallas import tpu as pltpu
from jax.sharding import PartitionSpec as P

MESH = pl.DeviceIdType.MESH
LANES = 128
DEPTHS = 4
AWAY = (0, 20, 21)


def kernel(
    sectors, slabs, times, fields, share, away,
    strip_src, state_src, visc_src, jac_src, freq_src, offs_src, total,
    state, strip, coeff, jac, freq, offs,
    edge_up, edge_down, from_up, from_down,
    edges, edges_left, edges_right,
    gathered, turned, ghost,
    load_sem, send_sem, recv_sem, ready_sem, home_sem,
):
    row = lax.axis_index("row")
    me = lax.axis_index("sec")
    slab = lax.axis_index("span")
    planes = times * fields
    cells = planes * 4
    annulus = sectors * LANES

    def is_holder(sector):
        held = sector != away[0]
        for other in away[1:]:
            held = held & (sector != other)
        return held

    def rank(sector):
        before = sector
        for other in away:
            before = before - jnp.where(sector > other, 1, 0)
        return before

    is_home = is_holder(me)
    mine = rank(me)

    depth = lax.rem(slab, DEPTHS)
    ordered = depth == DEPTHS - 1
    is_root = (row == 0) & (me == 0) & (slab == 0)

    def lateness(at_row, sector):
        along = sector & 7
        late = 10 * jnp.minimum(along, 8 - along) + jnp.where(along > 3, 10, 0) + 60 * (sector >> 3)
        return late * (2 * sectors) + 2 * sector + at_row

    here = lateness(row, me)

    def root_at(at_row, sector):
        return (at_row == 0) & (sector == 0) & (slab == 0)

    targets = [lax.rem(me + step, sectors) for step in range(sectors)]
    held = [is_holder(target) for target in targets]
    far_first = sorted(range(sectors), key=lambda step: -min(step % 8, 8 - step % 8))

    def choose(one, other):
        return (ordered & one) | (~ordered & other)

    across_later = [ordered & (lateness(1 - row, target) > here) for target in targets]
    along_later = [lateness(row, target) > here for target in targets]
    across_greet = [choose(later, is_home) for later in across_later]
    across_wait = [choose(~later, at) for later, at in zip(across_later, held)]
    along_greet, along_wait, along_tell, along_miss = [None], [None], [None], [None]
    for step in range(1, sectors):
        later, at = along_later[step], held[step]
        greet, wait = is_home & ~at, ~is_home & at
        if step in (1, sectors - 1):
            greet, wait = greet | ~is_root, wait | ~root_at(row, targets[step])
        along_greet.append(choose(later, greet))
        along_wait.append(choose(~later, wait))
        along_tell.append(choose(~later & at, ~is_home & at))
        along_miss.append(choose(later, is_home & ~at))

    has_up = slab < slabs - 1
    has_down = slab > 0
    up_later = has_up & (depth != DEPTHS - 1) & ~is_root
    up_earlier = has_up & ~up_later
    down_later = has_down & ((depth == 0) | ((row == 0) & (me == 0) & (slab == 1)))
    down_earlier = has_down & ~down_later

    def beside(step):
        root, later = root_at(row, targets[step]), along_later[step]
        return choose(~later, ~root), choose(~later, is_root), choose(later, root)

    neighbours = (
        (up_earlier, up_earlier, up_later, {"span": slab + 1}, 0, 1),
        (down_earlier, down_earlier, down_later, {"span": slab - 1}, 1, 0),
        (*beside(1), {"sec": targets[1]}, 2, 3),
        (*beside(sectors - 1), {"sec": targets[sectors - 1]}, 3, 2),
    )

    barrier = pltpu.get_barrier_semaphore()

    def signal(sem, device):
        pl.semaphore_signal(sem, inc=1, device_id=device, device_id_type=MESH)

    def count(flags):
        return sum(flag.astype(jnp.int32) for flag in flags)

    for step in far_first:
        pl.when(across_greet[step])(
            functools.partial(signal, barrier, {"row": 1 - row, "sec": targets[step]})
        )
    for step in far_first:
        if step:
            pl.when(along_greet[step])(
                functools.partial(signal, barrier, {"sec": targets[step]})
            )
    for _, _, later, device, _, _ in neighbours[:2]:
        pl.when(later)(functools.partial(signal, barrier, device))

    planes_load = pltpu.make_async_copy(strip_src.at[:, 3], strip, load_sem.at[5])
    planes_load.start()
    loads = (
        pltpu.make_async_copy(state_src, state, load_sem.at[0]),
        pltpu.make_async_copy(visc_src, coeff, load_sem.at[1]),
        pltpu.make_async_copy(jac_src, jac, load_sem.at[2]),
        pltpu.make_async_copy(freq_src, freq, load_sem.at[3]),
        pltpu.make_async_copy(offs_src, offs, load_sem.at[4]),
    )
    for load in loads:
        load.start()

    pl.semaphore_wait(
        barrier, count(across_wait + along_wait[1:] + [up_earlier, down_earlier])
    )
    planes_load.wait()
    for _, told, _, device, _, there in neighbours:
        pl.when(told)(functools.partial(signal, ready_sem.at[there], device))

    def spread(chosen):
        for step in far_first:

            @pl.when(held[step] & chosen[step])
            def _(target=targets[step]):
                pltpu.make_async_remote_copy(
                    src_ref=strip.at[pl.ds(share * rank(target), share)],
                    dst_ref=gathered.at[me],
                    send_sem=send_sem.at[0],
                    recv_sem=recv_sem.at[0],
                    device_id={"row": 1 - row, "sec": target},
                    device_id_type=MESH,
                ).start()

    @pl.when(is_home & ordered)
    def _():
        for step in far_first:
            pl.when(~across_later[step])(
                functools.partial(
                    signal, home_sem.at[0], {"row": 1 - row, "sec": targets[step]}
                )
            )

    spread([~later for later in across_later])
    for step in range(1, sectors):
        pl.when(along_tell[step])(
            functools.partial(signal, home_sem.at[1], {"sec": targets[step]})
        )

    for load in loads:
        load.wait()

    edge_up[...] = state[pl.ds(3, cells, stride=4), :]
    edge_down[...] = state[pl.ds(0, cells, stride=4), :]
    to_right = pltpu.make_async_remote_copy(
        src_ref=edges, dst_ref=edges_left, send_sem=send_sem.at[1], recv_sem=recv_sem.at[1],
        device_id={"sec": targets[1]}, device_id_type=MESH,
    )
    to_left = pltpu.make_async_remote_copy(
        src_ref=edges, dst_ref=edges_right, send_sem=send_sem.at[2], recv_sem=recv_sem.at[2],
        device_id={"sec": targets[sectors - 1]}, device_id_type=MESH,
    )
    to_up = pltpu.make_async_remote_copy(
        src_ref=edge_up, dst_ref=from_down, send_sem=send_sem.at[3], recv_sem=recv_sem.at[3],
        device_id={"span": slab + 1}, device_id_type=MESH,
    )
    to_down = pltpu.make_async_remote_copy(
        src_ref=edge_down, dst_ref=from_up, send_sem=send_sem.at[4], recv_sem=recv_sem.at[4],
        device_id={"span": slab - 1}, device_id_type=MESH,
    )
    halos = tuple(zip((to_up, to_down, to_right, to_left), neighbours))
    for halo, (earlier, _, _, _, _, _) in halos[:2]:
        pl.when(earlier)(halo.start)

    lane = lax.broadcasted_iota(jnp.int32, (8, LANES), 1)
    sub = lax.broadcasted_iota(jnp.int32, (8, LANES), 0)

    def rows_of(t, f, half):
        return pl.ds(pl.multiple_of(t * (fields * 16) + (f * 16 + half * 8), 8), 8)

    def pack(t, held):
        packed = []
        for half in range(2):
            part = jnp.zeros((8, LANES), jnp.float32)
            for f in range(fields):
                turn = pltpu.roll(state[rows_of(t, f, half), :], 2 * f + 1, 1)
                part = jnp.where((lane >> 1) == f, turn, part)
            packed.append(held[half] + pltpu.roll(part, t * (2 * fields), 1))
        return tuple(packed)

    zero = jnp.zeros((8, LANES), jnp.float32)
    packed = lax.fori_loop(0, times, pack, (zero, zero))
    edges[pl.ds(0, 8), :] = packed[0]
    edges[pl.ds(8, 8), :] = packed[1]

    for halo, (earlier, _, _, _, _, _) in halos[2:]:
        pl.when(earlier)(halo.start)

    weights = [
        freq[0] * jnp.float32(-0.05 * (-1.0) ** m / math.sin(math.pi * m / times))
        for m in range(1, times // 2 + 1)
    ]

    @pl.loop(0, fields)
    def _(f):
        for half in range(2):
            at = [
                pl.ds(pl.multiple_of(f * 16 + (t * fields * 16 + half * 8), 8), 8)
                for t in range(times)
            ]
            values = [state[at[t], :] for t in range(times)]
            for t in range(times):
                acc = None
                for m, weight in enumerate(weights, 1):
                    term = weight * (values[(t - m) % times] - values[(t + m) % times])
                    acc = term if acc is None else acc + term
                total[at[t], :] = acc

    def send_later(index, now):
        halo, (_, _, later, _, told, _) = halos[index]

        @pl.when(later & now)
        def _():
            pl.semaphore_wait(ready_sem.at[told], 1)
            halo.start()

    across = count([later & at for later, at in zip(across_later, held)])

    @pl.when(across > 0)
    def _():
        pl.semaphore_wait(home_sem.at[0], across)
        spread(across_later)

    beside_root = (row == 0) & (slab == 0)
    root_right = beside_root & (targets[1] == 0)
    root_left = beside_root & (targets[sectors - 1] == 0)
    send_later(2, ~root_right)
    send_later(3, ~root_left)
    soon = (depth == DEPTHS - 2) | (depth == DEPTHS - 3)
    send_later(0, soon)

    @pl.when(is_home)
    def _():
        pltpu.make_async_copy(gathered, gathered, recv_sem.at[0]).wait()
        along = count(along_miss[1:])

        @pl.when(along > 0)
        def _():
            pl.semaphore_wait(home_sem.at[1], along)

        thin = lax.broadcasted_iota(jnp.int32, (4, LANES), 1)
        wholes, rests = [], []
        for part in range(share):
            offset = offs[(share * mine + part) // fields]
            shift = jnp.where(row == 0, offset, annulus - offset)
            wholes.append(shift >> 7)
            rests.append(shift & (LANES - 1))

        def source(sector, part):
            at = lax.rem(sector + (2 * sectors - wholes[part]), sectors)
            return pltpu.roll(gathered[at, part], rests[part], 1)

        before = [source(me - 1, part) for part in range(share)]
        there = ghost.at[pl.ds(share * mine, share)]
        for step in range(sectors):
            target = lax.rem(me + step, sectors)
            for part in range(share):
                after = source(me + step, part)
                turned[target, part] = jnp.where(thin >= rests[part], after, before[part])
                before[part] = after
            if step == 0:
                pltpu.make_async_copy(turned.at[me], there, recv_sem.at[5]).start()
            else:
                pltpu.make_async_remote_copy(
                    src_ref=turned.at[target],
                    dst_ref=there,
                    send_sem=send_sem.at[5],
                    recv_sem=recv_sem.at[5],
                    device_id={"sec": target},
                    device_id_type=MESH,
                ).start()

    send_later(2, root_right)
    send_later(3, root_left)
    send_later(1, has_down)
    send_later(0, ~soon)

    to_right.wait_recv()
    to_left.wait_recv()
    mix = [[jac[f, 0, g] * jnp.float32(-0.05) for g in range(fields)] for f in range(fields)]
    diffuse = [coeff[pl.ds(8 * half, 8), :] * jnp.float32(0.1) for half in range(2)]
    first_span = (sub & 3) == 0
    last_span = (sub & 3) == 3
    low = sub < 4

    @pl.loop(0, times)
    def _(t):
        turn = lax.rem(LANES - t * (2 * fields), LANES)
        lefts = [pltpu.roll(edges_left[pl.ds(8 * h, 8), :], turn, 1) for h in range(2)]
        rights = [pltpu.roll(edges_right[pl.ds(8 * h, 8), :], turn, 1) for h in range(2)]
        slopes = []
        for f in range(fields):
            pair = [state[rows_of(t, f, half), :] for half in range(2)]
            swapped = [pltpu.roll(v, 4, 0) for v in pair]
            middle = jnp.where(low, swapped[0], swapped[1])
            axial = (
                middle + jnp.where(low, 0.0, swapped[0]),
                middle + jnp.where(low, swapped[1], 0.0),
            )
            slope = []
            for half in range(2):
                v = pair[half]
                plus = jnp.where(
                    lane == LANES - 1,
                    pltpu.roll(rights[half], (LANES - 2 - 2 * f) % LANES, 1),
                    pltpu.roll(v, LANES - 1, 1),
                )
                minus = jnp.where(
                    lane == 0,
                    pltpu.roll(lefts[half], (LANES - 2 * f) % LANES, 1),
                    pltpu.roll(v, 1, 1),
                )
                around = plus + minus
                slope.append(plus - minus)
                around = around + jnp.where(last_span, 0.0, pltpu.roll(v, 7, 0))
                around = around + jnp.where(first_span, 0.0, pltpu.roll(v, 1, 0))
                at = rows_of(t, f, half)
                total[at, :] = (
                    total[at, :]
                    + 0.8 * v
                    + 0.1 * axial[half]
                    + diffuse[half] * (around - 4.0 * v)
                )
            slopes.append(slope)
        for f in range(fields):
            for half in range(2):
                acc = mix[f][0] * slopes[0][half]
                for g in range(1, fields):
                    acc = acc + mix[f][g] * slopes[g][half]
                at = rows_of(t, f, half)
                total[at, :] = total[at, :] + acc

    def span_weights(s):
        rows = [coeff[pl.ds(4 * a + s, 1), :] * jnp.float32(0.1) for a in range(4)]
        out = jnp.broadcast_to(rows[3], (8, LANES))
        for a in range(3):
            out = jnp.where((sub & 3) == a, jnp.broadcast_to(rows[a], (8, LANES)), out)
        return out

    def add_span(source, s):
        weight = span_weights(s)
        whole = cells // 8
        for block in range(whole):
            at = pl.ds(block * 32 + s, 8, stride=4)
            total[at, :] = total[at, :] + weight * source[pl.ds(block * 8, 8), :]
        if cells % 8:
            at = pl.ds(whole * 32 + s, cells % 8, stride=4)
            total[at, :] = (
                total[at, :]
                + weight[: cells % 8] * source[pl.ds(whole * 8, cells % 8), :]
            )

    @pl.when(has_up)
    def _():
        to_down.wait_recv()
        add_span(from_up, 3)

    @pl.when(has_down)
    def _():
        to_up.wait_recv()
        add_span(from_down, 0)

    pltpu.make_async_copy(ghost, ghost, recv_sem.at[5]).wait()
    for n in range(planes):
        at = pl.ds(16 * n + 12, 4)
        total[at, :] = total[at, :] + 0.1 * ghost[n]

    pltpu.make_async_copy(ghost, ghost, send_sem.at[0]).wait()
    to_right.wait_send()
    to_left.wait_send()

    @pl.when(has_up)
    def _():
        to_up.wait_send()

    @pl.when(has_down)
    def _():
        to_down.wait_send()

    @pl.when(is_home)
    def _():
        others = turned.at[pl.ds(0, sectors - 1)]
        pltpu.make_async_copy(others, others, send_sem.at[5]).wait()


def solution(mesh):
    sectors, slabs = mesh.shape["sec"], mesh.shape["span"]

    def on_device(state, viscosity, jacobian, frequency, offsets):
        _, times, fields, axial, span, lanes = state.shape
        planes = times * fields
        share = planes // (sectors - len(AWAY))
        rows = planes * axial * span
        edge = pltpu.VMEM((planes * axial, lanes), jnp.float32)
        pairs = pltpu.VMEM((16, lanes), jnp.float32)
        anywhere = pl.BlockSpec(memory_space=pltpu.HBM)
        out = pl.pallas_call(
            functools.partial(kernel, sectors, slabs, times, fields, share, AWAY),
            out_shape=pltpu.VMEM((rows, lanes), jnp.float32),
            in_specs=[anywhere] * 6,
            out_specs=pl.BlockSpec(memory_space=pltpu.VMEM),
            scratch_shapes=[
                pltpu.VMEM((rows, lanes), jnp.float32),
                pltpu.VMEM((planes, span, lanes), jnp.float32),
                pltpu.VMEM((16, lanes), jnp.float32),
                pltpu.SMEM((fields, 1, fields), jnp.float32),
                pltpu.SMEM((1,), jnp.float32),
                pltpu.SMEM((times,), jnp.int32),
                edge, edge, edge, edge,
                pairs, pairs, pairs,
                pltpu.VMEM((sectors, share, span, lanes), jnp.float32),
                pltpu.VMEM((sectors, share, span, lanes), jnp.float32),
                pltpu.VMEM((planes, span, lanes), jnp.float32),
                pltpu.SemaphoreType.DMA((6,)),
                pltpu.SemaphoreType.DMA((6,)),
                pltpu.SemaphoreType.DMA((6,)),
                pltpu.SemaphoreType.REGULAR((4,)),
                pltpu.SemaphoreType.REGULAR((2,)),
            ],
            compiler_params=pltpu.CompilerParams(collective_id=0, has_side_effects=True),
        )(
            state.reshape(planes, axial, span, lanes),
            state.reshape(rows, lanes),
            viscosity.reshape(axial * span, lanes),
            jacobian.reshape(fields, 1, fields),
            frequency,
            offsets,
        )
        return out.reshape(state.shape)

    return jax.shard_map(
        on_device,
        mesh=mesh,
        in_specs=(
            P("row", None, None, None, "span", "sec"),
            P("row", None, "span", "sec"),
            P("row", None, None),
            P("row"),
            P(),
        ),
        out_specs=P("row", None, None, None, "span", "sec"),
        check_vma=False,
    )
```
